32 devices in a mesh: det: 8 (over y, x, core), row: 4 (over z).
Axes of the slice: x: 2, y: 2, z: 4, core: 2. Of those that a mesh axis runs over, the one named last changes fastest.
Arguments:
- coefficients: bfloat16 [8, 2048, 200], P('det', 'row'), may hold values from -1 to 1
- amplitudes: bfloat16 [8], P('det'), may hold values from -3 to 3
- plan: int32 [8, 2, 1], P('det'), may hold values 0 or 1
Outputs:
- density: float32 [2048, 2048], P('det', 'row')
The draws below stay inside these ranges and needn't reach their ends.
All inputs are finite; a program needn't handle non-finite values. No bound on the sum of `plan` on one device may be relied on, other than what follows from the above.
Results may differ from the reference program's by a relative error of at most 0.0024.
Values may be sent and summed in bfloat16 or wider, within the bound.
A program may use at most 64 MiB of HBM per device.

```python
import math
import jax
import jax.numpy as jnp
from jax import lax

NB = 2048
NOCC = 200
DET_DEV = 1
STEPS = 2
ORDER = 2
NDETS = 8
N_DET = 8


def draw_coefficients(key, part):
    shared = jax.random.normal(jax.random.fold_in(key, 11), (NB, NOCC), jnp.float32)
    basis, unused = jnp.linalg.qr(shared)
    spread = math.sqrt(0.3 / NB)
    weight_basis = math.sqrt(0.55)
    noise = jax.random.normal(jax.random.fold_in(key, 12), (NDETS, NB, NOCC), jnp.float32)
    values = weight_basis * basis[None, :, :] + spread * noise
    return jnp.clip(values, -1.0, 1.0).astype(jnp.bfloat16)


def touch_ends(array, key, least, top_value):
    spot = [jax.random.randint(jax.random.fold_in(key, axis), (), 0, length) for axis, length in enumerate(array.shape)]
    widest = array.shape.index(max(array.shape))
    next_to = spot[:widest] + [(spot[widest] + 1) % array.shape[widest]] + spot[widest + 1:]
    return array.at[tuple(spot)].set(least).at[tuple(next_to)].set(top_value)


def steps_of(key, dims, split, least, largest):
    factor_of = 1.0
    for dim, blocks in split:
        steps = jax.random.uniform(jax.random.fold_in(jax.random.fold_in(key, 6), dim), (blocks,), jnp.float32, least / len(split), largest / len(split))
        factor_of = factor_of * jnp.repeat(jnp.exp(steps), dims[dim] // blocks).reshape((-1,) + (1,) * (len(dims) - 1 - dim))
    return factor_of


def scatter_about(key, dims, width, limit, pieces=(), kind=jnp.bfloat16):
    result = width * jax.random.normal(key, dims, jnp.float32)
    if pieces:
        result = result * steps_of(key, dims, pieces, -0.22, 0.18)
    return jnp.clip(result, -limit, limit).astype(kind)


def setup_inputs(seed: int = 0) -> dict:
    arg_keys = jax.random.split(jax.random.key(seed), 4)
    return {
        "coefficients": draw_coefficients(jax.random.fold_in(arg_keys[3], 71), 0),
        "amplitudes": scatter_about(arg_keys[1], (NDETS,), 0.5, 3.0, ((0, 8),)),
        "plan": touch_ends((jax.random.randint(arg_keys[2], (NDETS, STEPS, DET_DEV), 0, 2) < 1).astype(jnp.int32), jax.random.fold_in(arg_keys[2], 1), 0, 1),
    }


def neumann(correlation):
    identity = jnp.eye(correlation.shape[-1], dtype=jnp.float32)
    remainder = identity - correlation
    inverse = identity + jnp.zeros_like(correlation)
    for level in range(ORDER):
        inverse = identity + jnp.einsum('...ab,...bc->...ac', remainder, inverse, precision=lax.Precision.HIGHEST)
    return inverse

def reference(coefficients, amplitudes, plan):
    blocks = coefficients.reshape(N_DET, DET_DEV, NB, NOCC)
    block_amps = amplitudes.astype(jnp.float32).reshape(N_DET, DET_DEV)
    masks = plan.astype(jnp.float32).reshape(N_DET, DET_DEV, STEPS, DET_DEV)

    def visit(total, block):
        ket = lax.dynamic_index_in_dim(blocks, block, 0, keepdims=False).astype(jnp.float32)
        ket_amps = lax.dynamic_index_in_dim(block_amps, block, 0, keepdims=False)
        ket_masks = lax.dynamic_index_in_dim(masks, block, 0, keepdims=False)
        accum = jnp.zeros((DET_DEV, NOCC, NB), jnp.float32)
        for step in range(STEPS):
            source = ((block - step) % N_DET).astype(jnp.int32)
            visitor = lax.dynamic_index_in_dim(blocks, source, 0, keepdims=False).astype(jnp.float32)
            visitor_amps = lax.dynamic_index_in_dim(block_amps, source, 0, keepdims=False)
            correlation = jnp.einsum('ina,jnb->ijab', visitor, ket, precision=lax.Precision.HIGHEST)
            weight = visitor_amps[:, None] * ket_amps[None, :] * ket_masks[:, step, :].T
            scaled = (weight[:, :, None, None] * neumann(correlation)).astype(jnp.bfloat16)
            accum = accum + jnp.einsum('ijba,ina->jbn', scaled.astype(jnp.float32), visitor, precision=lax.Precision.HIGHEST)
        folded = accum.astype(jnp.bfloat16).astype(jnp.float32)
        total = total + jnp.einsum('jmb,jbn->mn', ket, folded, precision=lax.Precision.HIGHEST)
        return (total, None)
    total, unused = lax.scan(visit, jnp.zeros((NB, NB), jnp.float32), jnp.arange(N_DET, dtype=jnp.int32))
    return total
```

```python
import functools

import jax
import jax.numpy as jnp
from jax import lax
from jax.experimental import pallas as pl
from jax.experimental.pallas import tpu as pltpu
from jax.sharding import PartitionSpec as P

ORDER = 2
F32 = jnp.float32
BF16 = jnp.bfloat16


def each(count, body):
    if count <= 8:
        for i in range(count):
            body(i)
    else:
        lax.fori_loop(0, count, lambda i, c: (body(i), c)[1], 0)


def inverse_of(correlation):
    size = correlation.shape[0]
    row = lax.broadcasted_iota(jnp.int32, (size, size), 0)
    col = lax.broadcasted_iota(jnp.int32, (size, size), 1)
    identity = jnp.where(row == col, 1.0, 0.0).astype(F32)
    remainder = identity - correlation
    inverse = identity + remainder
    for level in range(ORDER - 1):
        inverse = identity + jnp.dot(
            remainder, inverse, precision=lax.Precision.HIGHEST, preferred_element_type=F32
        )
    return inverse


def gram(a, b):
    return lax.dot_general(a, b, (((0,), (0,)), ((), ())), preferred_element_type=F32)


def against(a, b):
    return lax.dot_general(a, b, (((1,), (1,)), ((), ())), preferred_element_type=F32)


def parts_of(size, count):
    step = -(-size // (8 * count)) * 8
    return [(start, min(step, size - start)) for start in range(0, size, step)]


def kernel(
    n, ring, c_ref, amp_ref, plan_ref, out_ref,
    cw, vis, amps, own, sum_in, sum_out, s0, pieces, folded, wide,
    local_sem, cw_send, cw_recv, sum_send, sum_recv, vis_send, vis_recv,
    piece_send, piece_recv, chip_send, pair_send, folded_recv,
):
    det = lax.axis_index("det")
    row = lax.axis_index("row")
    rows = out_ref.shape[0]
    width = pieces.shape[2]
    per_block = n // ring
    chips = n // 2
    chip, core = det // 2, lax.rem(det, 2)
    partner = chip * 2 + (1 - core)
    has_right, has_left = row < ring - 1, row > 0
    toward = (has_right, has_left)
    chunks = parts_of(own.shape[0], 4)

    def remote(src, dst, send, recv, **where):
        return pltpu.make_async_remote_copy(
            src_ref=src, dst_ref=dst, send_sem=send, recv_sem=recv,
            device_id=where, device_id_type=pl.DeviceIdType.MESH,
        )

    keep = pltpu.make_async_copy(c_ref, cw.at[row], local_sem)
    keep.start()

    barrier = pltpu.get_barrier_semaphore()

    def greet(i):
        peer = lax.rem(det + 1 + i, n)
        pl.semaphore_signal(barrier, inc=1, device_id={"det": peer}, device_id_type=pl.DeviceIdType.MESH)

    each(n - 1, greet)

    for side in (0, 1):

        @pl.when(toward[side])
        def _():
            peer = row + 1 - 2 * side
            pl.semaphore_signal(barrier, inc=1, device_id={"row": peer}, device_id_type=pl.DeviceIdType.MESH)

    amps[0] = jnp.broadcast_to(amp_ref[...].astype(F32), amps.shape[1:])
    pl.semaphore_wait(barrier, n - 1 + has_right.astype(jnp.int32) + has_left.astype(jnp.int32))

    halves = parts_of(own.shape[0], 2)

    def along(block, side, half):
        span = cw.at[block, pl.ds(*halves[half])]
        return remote(
            span, span, cw_send.at[block, side, half], cw_recv.at[block, half], row=row + 1 - 2 * side
        )

    def pass_on(block, side, half, wait=False):
        @pl.when(toward[side])
        def _():
            copy = along(block, side, half)
            if wait:
                copy.wait_send()
            else:
                copy.start()

    def chunk_copy(k, side):
        span = pl.ds(*chunks[k])
        return remote(
            sum_out.at[side, span], sum_in.at[side, span], sum_send.at[side, k], sum_recv.at[side, k],
            row=row + 1 - 2 * side,
        )

    def sums(side, first):
        for k, (start, length) in enumerate(chunks):
            span = pl.ds(start, length)
            if first:
                sum_in[side, span] = jnp.zeros((length, own.shape[1]), F32)
                sum_out[side, span] = own[span]
            else:
                chunk_copy(k, side).wait_recv()
                sum_out[side, span] = own[span] + sum_in[side, span]

            @pl.when(toward[side])
            def _():
                chunk_copy(k, side).start()

    def piece(block, k):
        target = block * per_block + k
        start = pl.multiple_of(k * rows // width * width, width)
        return target, remote(
            cw.at[block, :, pl.ds(start, width)], pieces.at[det],
            piece_send.at[block, k], piece_recv.at[det], det=target,
        )

    def hand_out(block, wait=False):
        def one(k):
            target, copy = piece(block, k)

            @pl.when(target != det)
            def _():
                if wait:
                    copy.wait_send()
                else:
                    copy.start()

        each(per_block, one)

    following = lax.rem(det + 1, n)
    visit = remote(c_ref, vis, vis_send.at[0], vis_recv.at[0], det=following)
    visit_amp = remote(amps.at[0], amps.at[1], vis_send.at[1], vis_recv.at[1], det=following)
    visit.start()
    visit_amp.start()
    keep.wait()
    for half in (0, 1):
        for side in (0, 1):
            pass_on(row, side, half)
    s0[...] = against(c_ref[...], c_ref[...])
    visit.wait_recv()
    own[...] = against(vis[...], c_ref[...])

    @pl.when(row == 0)
    def _():
        sums(0, True)

    @pl.when(row == ring - 1)
    def _():
        sums(1, True)

    hand_out(row)

    def arrive(distance):
        for side in (0, 1):
            block = row - distance if side == 0 else row + distance

            @pl.when((block >= 0) & (block < ring))
            def _():
                along(block, side, 0).wait_recv()
                pass_on(block, side, 0)

        for side in (0, 1):
            block = row - distance if side == 0 else row + distance

            @pl.when((block >= 0) & (block < ring))
            def _():
                along(block, side, 1).wait_recv()
                pass_on(block, side, 1)
                hand_out(block)
                s0[...] += against(cw[block], cw[block])

    def gather_sums(distance):
        @pl.when(row == distance)
        def _():
            sums(0, False)

        @pl.when(row == ring - 1 - distance)
        def _():
            sums(1, False)

    for distance in range(1, ring - 1):
        arrive(distance)
        gather_sums(distance)
    arrive(ring - 1)
    visit_amp.wait_recv()
    amp = amps[0, 0:1, 0:1]
    masks = plan_ref[...].astype(F32)
    weight = amp * amp * masks[0:1, 0:1]
    scaled = (weight * inverse_of(s0[...])).astype(BF16)
    total = jnp.dot(scaled, c_ref[...], preferred_element_type=F32)
    gather_sums(ring - 1)
    weight = amps[1, 0:1, 0:1] * amp * masks[0:1, 1:2]
    correlation = own[...] + sum_in[0] + sum_in[1]
    scaled = (weight * inverse_of(correlation)).astype(BF16)
    total = total + jnp.dot(scaled, vis[...], preferred_element_type=F32)
    folded[det] = total.astype(BF16)

    def to_chip(i):
        target = lax.rem(chip + 1 + i, chips) * 2 + core
        return remote(folded.at[det], folded.at[det], chip_send.at[i], folded_recv.at[det], det=target)

    def to_pair(source):
        return remote(
            folded.at[source], folded.at[source], pair_send.at[source], folded_recv.at[source], det=partner
        )

    each(chips - 1, lambda i: to_chip(i).start())
    to_pair(det).start()

    def landed(source):
        to_pair(source).wait_recv()

    sink = out_ref if width == rows else wide

    def add(source):
        remote(
            cw.at[0, :, pl.ds(0, width)], pieces.at[source], piece_send.at[0, 0], piece_recv.at[source],
            det=partner,
        ).wait_recv()
        sink[...] += gram(pieces[source], folded[source])

    own_start = lax.rem(det, per_block) * rows // width * width
    mine = cw[det // per_block, :, pl.ds(pl.multiple_of(own_start, width), width)]
    sink[...] = gram(mine, folded[det])
    landed(partner)
    add(partner)

    def relay(i):
        other = lax.rem(chip + chips - 1 - i, chips) * 2
        landed(other + core)
        to_pair(other + core).start()
        add(other + core)

    def relayed(i):
        other = lax.rem(chip + chips - 1 - i, chips) * 2
        landed(other + 1 - core)
        add(other + 1 - core)

    each(chips - 1, relay)
    each(chips - 1, relayed)
    if width != rows:
        out_ref[...] = wide[pl.ds(pl.multiple_of(lax.rem(det * rows, width), rows), rows)]

    visit.wait_send()
    visit_amp.wait_send()
    for side in (0, 1):
        for half in (0, 1):
            pass_on(row, side, half, wait=True)

        @pl.when(toward[side])
        def _():
            for k in range(len(chunks)):
                chunk_copy(k, side).wait_send()

    hand_out(row, wait=True)
    for distance in range(1, ring):
        for side in (0, 1):
            block = row - distance if side == 0 else row + distance

            @pl.when((block >= 0) & (block < ring))
            def _():
                for half in (0, 1):
                    pass_on(block, side, half, wait=True)
                hand_out(block, wait=True)

    each(chips - 1, lambda i: to_chip(i).wait_send())
    to_pair(det).wait_send()
    each(chips - 1, lambda i: to_pair(lax.rem(chip + chips - 1 - i, chips) * 2 + core).wait_send())


def on_device(coefficients, amplitudes, plan):
    n, ring = lax.axis_size("det"), lax.axis_size("row")
    if coefficients.shape[0] != 1 or plan.shape[1] != 2:
        raise ValueError("unsupported sizes")
    block = jnp.swapaxes(coefficients, 1, 2)[0]
    orbitals, size = block.shape
    rows = size * ring // n
    width = max(rows, 128)
    dma = pltpu.SemaphoreType.DMA
    lanes = -(-orbitals // 128) * 128
    used = 2 * orbitals * (size * (ring + 1 + n) + width * n) + 24 * orbitals * lanes + 4 * size * (rows + width)
    return pl.pallas_call(
        functools.partial(kernel, n, ring),
        out_shape=jax.ShapeDtypeStruct((rows, size), F32),
        in_specs=[pl.BlockSpec(memory_space=pltpu.VMEM)] * 3,
        out_specs=pl.BlockSpec(memory_space=pltpu.VMEM),
        scratch_shapes=[
            pltpu.VMEM((ring, orbitals, size), BF16),
            pltpu.VMEM((orbitals, size), BF16),
            pltpu.VMEM((2, 8, 128), F32),
            pltpu.VMEM((orbitals, orbitals), F32),
            pltpu.VMEM((2, orbitals, orbitals), F32),
            pltpu.VMEM((2, orbitals, orbitals), F32),
            pltpu.VMEM((orbitals, orbitals), F32),
            pltpu.VMEM((n, orbitals, width), BF16),
            pltpu.VMEM((n, orbitals, size), BF16),
            pltpu.VMEM((width, size) if width != rows else (8, 128), F32),
            dma, dma((ring, 2, 2)), dma((ring, 2)), dma((2, 4)), dma((2, 4)), dma((2,)), dma((2,)),
            dma((ring, n // ring)), dma((n,)), dma((n // 2,)), dma((n,)), dma((n,)),
        ],
        compiler_params=pltpu.CompilerParams(
            collective_id=0, has_side_effects=True, vmem_limit_bytes=used + 4 * 1024 * 1024
        ),
    )(block, amplitudes.reshape(1, 1), jnp.swapaxes(plan, 1, 2).reshape(1, 2))


def solution(mesh):
    placed = (P("det", "row", None), P("det"), P("det", None, None))
    return jax.shard_map(
        on_device, mesh=mesh, in_specs=placed, out_specs=P("det", "row"), check_vma=False
    )
```

```python
import functools

import jax
import jax.numpy as jnp
from jax import lax
from jax.experimental import pallas as pl
from jax.experimental.pallas import tpu as pltpu
from jax.sharding import PartitionSpec as P

ORDER = 2
F32 = jnp.float32
BF16 = jnp.bfloat16


def each(count, body):
    if count <= 8:
        for i in range(count):
            body(i)
    else:
        lax.fori_loop(0, count, lambda i, c: (body(i), c)[1], 0)


def inverse_of(correlation):
    size = correlation.shape[0]
    row = lax.broadcasted_iota(jnp.int32, (size, size), 0)
    col = lax.broadcasted_iota(jnp.int32, (size, size), 1)
    identity = jnp.where(row == col, 1.0, 0.0).astype(F32)
    remainder = identity - correlation
    inverse = identity + remainder
    for level in range(ORDER - 1):
        inverse = identity + jnp.dot(
            remainder, inverse, precision=lax.Precision.HIGHEST, preferred_element_type=F32
        )
    return inverse


def gram(a, b):
    return lax.dot_general(a, b, (((0,), (0,)), ((), ())), preferred_element_type=F32)


def against(a, b):
    return lax.dot_general(a, b, (((1,), (1,)), ((), ())), preferred_element_type=F32)


def parts_of(size, count):
    step = -(-size // (8 * count)) * 8
    return [(start, min(step, size - start)) for start in range(0, size, step)]


def swapped(det, index, n):
    if n & (n - 1):
        return lax.rem(det + index, n)
    bit, other = 1, det
    while bit < n:
        flip = lax.rem(index // bit, 2) * bit if not isinstance(index, int) else index // bit % 2 * bit
        other = other + flip * (1 - 2 * lax.rem(det // bit, 2))
        bit *= 2
    return other


def kernel(
    n, ring, c_ref, amp_ref, plan_ref, out_ref,
    vis, amps, own, sum_in, sum_out, pieces, folded, wide,
    local_sem, sum_send, sum_recv, vis_send, vis_recv,
    piece_send, piece_recv, pass_send, chip_send, pair_send, folded_recv,
):
    det = lax.axis_index("det")
    row = lax.axis_index("row")
    rows = out_ref.shape[0]
    width = pieces.shape[2]
    per_block = n // ring
    chips = n // 2
    chip, core = det // 2, lax.rem(det, 2)
    partner = chip * 2 + (1 - core)
    home = det // per_block
    toward = (row < ring - 1, row > 0)
    passes = ((row < ring - 1) & (row >= home), (row > 0) & (row <= home))
    relays = passes[0] | passes[1]
    steps_away = jnp.abs(row - home)
    chunks = parts_of(own.shape[1], 4)

    def remote(src, dst, send, recv, **where):
        return pltpu.make_async_remote_copy(
            src_ref=src, dst_ref=dst, send_sem=send, recv_sem=recv,
            device_id=where, device_id_type=pl.DeviceIdType.MESH,
        )

    def columns_of(target):
        start = lax.rem(target, per_block) * rows // width * width
        return c_ref.at[:, pl.ds(pl.multiple_of(start, width), width)]

    barrier = pltpu.get_barrier_semaphore()

    def greet(i):
        peer = lax.rem(det + 1 + i, n)
        pl.semaphore_signal(barrier, inc=1, device_id={"det": peer}, device_id_type=pl.DeviceIdType.MESH)

    each(n - 1, greet)

    for side in (0, 1):

        @pl.when(toward[side])
        def _():
            peer = row + 1 - 2 * side
            pl.semaphore_signal(barrier, inc=1, device_id={"row": peer}, device_id_type=pl.DeviceIdType.MESH)

    @pl.when(row == home)
    def _():
        keep = pltpu.make_async_copy(columns_of(det), pieces.at[det], local_sem)
        keep.start()
        keep.wait()

    amps[0] = jnp.broadcast_to(amp_ref[...].astype(F32), amps.shape[1:])
    own[0] = against(c_ref[...], c_ref[...])
    pl.semaphore_wait(barrier, n - 1 + toward[0].astype(jnp.int32) + toward[1].astype(jnp.int32))

    def chunk_copy(which, k, side):
        span = pl.ds(*chunks[k])
        return remote(
            sum_out.at[which, side, span], sum_in.at[which, side, span],
            sum_send.at[which, side, k], sum_recv.at[which, side, k], row=row + 1 - 2 * side,
        )

    def sums(which, side, first):
        for k, (start, length) in enumerate(chunks):
            span = pl.ds(start, length)
            if first:
                sum_in[which, side, span] = jnp.zeros((length, own.shape[2]), F32)
            else:
                chunk_copy(which, k, side).wait_recv()

            @pl.when(toward[side])
            def _():
                if first:
                    sum_out[which, side, span] = own[which, span]
                else:
                    sum_out[which, side, span] = own[which, span] + sum_in[which, side, span]
                chunk_copy(which, k, side).start()

    def gather_sums(which, distance):
        @pl.when(row == distance)
        def _():
            sums(which, 0, distance == 0)

        @pl.when(row == ring - 1 - distance)
        def _():
            sums(which, 1, distance == 0)

    def piece(k):
        target = row * per_block + k
        return target, remote(
            columns_of(target), pieces.at[det], piece_send.at[k], piece_recv.at[det], det=target
        )

    def hand_out(k, wait=False):
        target, copy = piece(k)

        @pl.when(target != det)
        def _():
            if wait:
                copy.wait_send()
            else:
                copy.start()

    def pass_copy(source, side):
        return remote(
            pieces.at[source], pieces.at[source], pass_send.at[source, side], piece_recv.at[source],
            row=row + 1 - 2 * side,
        )

    def pass_on(index):
        source = swapped(det, index, n)

        @pl.when(relays & (index >= 0) & (index < n))
        def _():
            @pl.when((row != home) | (source != det))
            def _():
                pass_copy(source, 0).wait_recv()

            for side in (0, 1):

                @pl.when(passes[side])
                def _():
                    pass_copy(source, side).start()

    share = max(n // 4, 1)

    def slot(number):
        each(share, lambda i: pass_on((number - steps_away) * share + i))

    following = lax.rem(det + 1, n)
    visit = remote(c_ref, vis, vis_send.at[0], vis_recv.at[0], det=following)
    visit_amp = remote(amps.at[0], amps.at[1], vis_send.at[1], vis_recv.at[1], det=following)
    visit.start()
    visit_amp.start()
    gather_sums(0, 0)
    each(per_block, hand_out)
    slot(0)
    visit.wait_recv()
    own[1] = against(vis[...], c_ref[...])
    gather_sums(1, 0)
    for distance in range(1, ring - 1):
        gather_sums(0, distance)
        gather_sums(1, distance)
        slot(distance)
    visit_amp.wait_recv()
    amp = amps[0, 0:1, 0:1]
    masks = plan_ref[...].astype(F32)
    gather_sums(0, ring - 1)
    weight = amp * amp * masks[0:1, 0:1]
    scaled = (weight * inverse_of(own[0] + sum_in[0, 0] + sum_in[0, 1])).astype(BF16)
    total = jnp.dot(scaled, c_ref[...], preferred_element_type=F32)
    gather_sums(1, ring - 1)
    weight = amps[1, 0:1, 0:1] * amp * masks[0:1, 1:2]
    scaled = (weight * inverse_of(own[1] + sum_in[1, 0] + sum_in[1, 1])).astype(BF16)
    total = total + jnp.dot(scaled, vis[...], preferred_element_type=F32)
    folded[det] = total.astype(BF16)

    def to_chip(i):
        target = swapped(chip, i + 1, chips) * 2 + core
        return remote(folded.at[det], folded.at[det], chip_send.at[i], folded_recv.at[det], det=target)

    def to_pair(source):
        return remote(
            folded.at[source], folded.at[source], pair_send.at[source], folded_recv.at[source], det=partner
        )

    each(chips - 1, lambda i: to_chip(i).start())
    to_pair(det).start()
    slots = -(-n // share) + ring - 2
    for number in range(ring - 1, slots):
        slot(number)

    sink = out_ref if width == rows else wide

    def add(source, first=False):
        @pl.when(jnp.logical_not(relays))
        def _():
            pass_copy(source, 0).wait_recv()

        value = gram(pieces[source], folded[source])
        sink[...] = value if first else sink[...] + value

    def landed(source):
        to_pair(source).wait_recv()

    add(det, True)
    landed(partner)
    add(partner)

    def relay(i):
        other = swapped(chip, i + 1, chips) * 2
        landed(other + core)
        to_pair(other + core).start()
        add(other + core)

    def relayed(i):
        other = swapped(chip, i + 1, chips) * 2
        landed(other + 1 - core)
        add(other + 1 - core)

    each(chips - 1, relay)
    each(chips - 1, relayed)
    if width != rows:
        out_ref[...] = wide[pl.ds(pl.multiple_of(lax.rem(det * rows, width), rows), rows)]

    visit.wait_send()
    visit_amp.wait_send()
    for side in (0, 1):

        @pl.when(toward[side])
        def _():
            for which in (0, 1):
                for k in range(len(chunks)):
                    chunk_copy(which, k, side).wait_send()

        @pl.when(passes[side])
        def _():
            each(n, lambda source: pass_copy(source, side).wait_send())

    each(per_block, lambda k: hand_out(k, wait=True))
    each(chips - 1, lambda i: to_chip(i).wait_send())
    to_pair(det).wait_send()
    each(chips - 1, lambda i: to_pair(swapped(chip, i + 1, chips) * 2 + core).wait_send())


def on_device(coefficients, amplitudes, plan):
    n, ring = lax.axis_size("det"), lax.axis_size("row")
    if coefficients.shape[0] != 1 or plan.shape[1] != 2:
        raise ValueError("unsupported sizes")
    block = jnp.swapaxes(coefficients, 1, 2)[0]
    orbitals, size = block.shape
    rows = size * ring // n
    width = max(rows, 128)
    dma = pltpu.SemaphoreType.DMA
    lanes = -(-orbitals // 128) * 128
    used = 2 * orbitals * (size * (ring + 1 + n) + width * n) + 40 * orbitals * lanes + 4 * size * (rows + width)
    return pl.pallas_call(
        functools.partial(kernel, n, ring),
        out_shape=jax.ShapeDtypeStruct((rows, size), F32),
        in_specs=[pl.BlockSpec(memory_space=pltpu.VMEM)] * 3,
        out_specs=pl.BlockSpec(memory_space=pltpu.VMEM),
        scratch_shapes=[
            pltpu.VMEM((orbitals, size), BF16),
            pltpu.VMEM((2, 8, 128), F32),
            pltpu.VMEM((2, orbitals, orbitals), F32),
            pltpu.VMEM((2, 2, orbitals, orbitals), F32),
            pltpu.VMEM((2, 2, orbitals, orbitals), F32),
            pltpu.VMEM((n, orbitals, width), BF16),
            pltpu.VMEM((n, orbitals, size), BF16),
            pltpu.VMEM((width, size) if width != rows else (8, 128), F32),
            dma, dma((2, 2, 4)), dma((2, 2, 4)), dma((2,)), dma((2,)),
            dma((n // ring,)), dma((n,)), dma((n, 2)), dma((n // 2,)), dma((n,)), dma((n,)),
        ],
        compiler_params=pltpu.CompilerParams(
            collective_id=0, has_side_effects=True, vmem_limit_bytes=used + 4 * 1024 * 1024
        ),
    )(block, amplitudes.reshape(1, 1), jnp.swapaxes(plan, 1, 2).reshape(1, 2))


def solution(mesh):
    placed = (P("det", "row", None), P("det"), P("det", None, None))
    return jax.shard_map(
        on_device, mesh=mesh, in_specs=placed, out_specs=P("det", "row"), check_vma=False
    )
```

```python
import functools

import jax
import jax.numpy as jnp
from jax import lax
from jax.experimental import pallas as pl
from jax.experimental.pallas import tpu as pltpu
from jax.sharding import PartitionSpec as P

ORDER = 2
F32 = jnp.float32
BF16 = jnp.bfloat16


def each(count, body):
    if count <= 8:
        for i in range(count):
            body(i)
    else:
        lax.fori_loop(0, count, lambda i, c: (body(i), c)[1], 0)


def inverse_of(correlation):
    size = correlation.shape[0]
    row = lax.broadcasted_iota(jnp.int32, (size, size), 0)
    col = lax.broadcasted_iota(jnp.int32, (size, size), 1)
    identity = jnp.where(row == col, 1.0, 0.0).astype(F32)
    remainder = identity - correlation
    inverse = identity + remainder
    for level in range(ORDER - 1):
        inverse = identity + jnp.dot(
            remainder, inverse, precision=lax.Precision.HIGHEST, preferred_element_type=F32
        )
    return inverse


def gram(a, b):
    return lax.dot_general(a, b, (((0,), (0,)), ((), ())), preferred_element_type=F32)


def against(a, b):
    return lax.dot_general(a, b, (((1,), (1,)), ((), ())), preferred_element_type=F32)


def parts_of(size, count):
    step = -(-size // (8 * count)) * 8
    return [(start, min(step, size - start)) for start in range(0, size, step)]


def splits(n, ring, size):
    halves = 2 if (n // ring) % 2 == 0 and size % 256 == 0 else 1
    chunks = 2 * halves if size % (256 * halves) == 0 else halves
    return chunks, halves


def kernel(
    n, ring, c_ref, amp_ref, plan_ref, out_ref,
    cw, vw, vis, amps, amp_in, plan_in, own, sum_in, sum_out, s0, pieces, folded, wide,
    local_sem, cw_send, cw_recv, vw_send, vw_recv, sum_send, sum_recv, vis_send, vis_recv,
    piece_send, piece_recv, near_send, relay_send, pair_send, folded_recv,
):
    det = lax.axis_index("det")
    row = lax.axis_index("row")
    rows, size = out_ref.shape
    width = pieces.shape[2]
    per_block = n // ring
    chips = n // 2
    chip, core = det // 2, lax.rem(det, 2)
    partner = chip * 2 + (1 - core)
    even = core == 0
    toward = (row < ring - 1, row > 0)
    sum_parts = parts_of(own.shape[0], 4)
    n_chunks, n_halves = splits(n, ring, size)
    chunk, half_size = size // n_chunks, size // n_halves

    def remote(src, dst, send, recv, **where):
        return pltpu.make_async_remote_copy(
            src_ref=src, dst_ref=dst, send_sem=send, recv_sem=recv,
            device_id=where, device_id_type=pl.DeviceIdType.MESH,
        )

    stage = [
        pltpu.make_async_copy(c_ref, cw.at[row], local_sem.at[0]),
        pltpu.make_async_copy(amp_ref, amp_in, local_sem.at[1]),
        pltpu.make_async_copy(plan_ref, plan_in, local_sem.at[2]),
    ]
    for copy in stage:
        copy.start()

    barrier = pltpu.get_barrier_semaphore()

    def greet(i):
        peer = lax.rem(det + 1 + i, n)
        pl.semaphore_signal(barrier, inc=1, device_id={"det": peer}, device_id_type=pl.DeviceIdType.MESH)

    each(n - 1, greet)

    for side in (0, 1):

        @pl.when(toward[side])
        def _():
            peer = row + 1 - 2 * side
            pl.semaphore_signal(barrier, inc=1, device_id={"row": peer}, device_id_type=pl.DeviceIdType.MESH)

    for copy in stage:
        copy.wait()
    amps[0] = jnp.broadcast_to(amp_in[...].astype(F32), amps.shape[1:])
    s0[...] = against(cw[row], cw[row])
    pl.semaphore_wait(barrier, n - 1 + toward[0].astype(jnp.int32) + toward[1].astype(jnp.int32))

    def along(block, side, q):
        span = cw.at[block, :, pl.ds(q * chunk, chunk)]
        return remote(
            span, span, cw_send.at[block, side, q], cw_recv.at[block, q], row=row + 1 - 2 * side
        )

    def pass_on(block, side, q, wait=False):
        @pl.when(toward[side])
        def _():
            copy = along(block, side, q)
            if wait:
                copy.wait_send()
            else:
                copy.start()

    def sum_copy(k, side):
        span = pl.ds(*sum_parts[k])
        return remote(
            sum_out.at[side, span], sum_in.at[side, span], sum_send.at[side, k], sum_recv.at[side, k],
            row=row + 1 - 2 * side,
        )

    def sums(side, first):
        for k, (start, length) in enumerate(sum_parts):
            span = pl.ds(start, length)
            if not first:
                sum_copy(k, side).wait_recv()

            @pl.when(toward[side])
            def _():
                if first:
                    sum_out[side, span] = own[span]
                else:
                    sum_out[side, span] = own[span] + sum_in[side, span]
                sum_copy(k, side).start()

    def gather_sums(distance):
        @pl.when(even & (row == distance))
        def _():
            sums(0, distance == 0)

        @pl.when(even & (row == ring - 1 - distance))
        def _():
            sums(1, distance == 0)

    def piece(block, k):
        target = block * per_block + k
        start = pl.multiple_of(k * rows // width * width, width)
        return target, remote(
            cw.at[block, :, pl.ds(start, width)], pieces.at[det],
            piece_send.at[block, k], piece_recv.at[det], det=target,
        )

    def hand_out(block, half, wait=False):
        share = per_block // n_halves

        def one(i):
            target, copy = piece(block, half * share + i)

            @pl.when(target != det)
            def _():
                if wait:
                    copy.wait_send()
                else:
                    copy.start()

        each(share, one)

    def columns(ref, block, half):
        return ref[block, :, pl.ds(half * half_size, half_size)]

    def to_partner(block, half):
        span = pl.ds(half * half_size, half_size)
        return remote(
            cw.at[block, :, span], vw.at[block, :, span], vw_send.at[block, half], vw_recv.at[block, half],
            det=partner,
        )

    following = lax.rem(det + 1, n)
    visit = remote(cw.at[row], vis, vis_send.at[0], vis_recv.at[0], det=following)
    visit_amp = remote(amps.at[0], amps.at[1], vis_send.at[1], vis_recv.at[1], det=following)
    visit.start()
    visit_amp.start()
    for q in range(n_chunks):
        for side in (0, 1):
            pass_on(row, side, q)
    for half in range(n_halves):
        hand_out(row, half)
    visit.wait_recv()
    own[...] = against(vis[...], cw[row])
    gather_sums(0)

    def blocks_at(distance):
        for side in (0, 1):
            block = row - distance if side == 0 else row + distance
            yield side, block, (block >= 0) & (block < ring)

    def arrive(distance):
        for q in range(n_chunks):
            for side, block, there in blocks_at(distance):

                @pl.when(there)
                def _():
                    along(block, side, q).wait_recv()
                    pass_on(block, side, q)
                    if (q + 1) % (n_chunks // n_halves) == 0:
                        half = q // (n_chunks // n_halves)

                        @pl.when(even)
                        def _():
                            to_partner(block, half).start()

                        hand_out(block, half)
                        part = columns(cw, block, half)
                        s0[...] += against(part, part)

    def visited(distance):
        for half in range(n_halves):
            for side, block, there in blocks_at(distance):

                @pl.when(there & jnp.logical_not(even))
                def _():
                    to_partner(block, half).wait_recv()
                    own[...] += against(columns(vw, block, half), columns(cw, block, half))

    for distance in range(1, ring):
        arrive(distance)
        if distance < ring - 1:
            visited(distance)
            gather_sums(distance)
    visit_amp.wait_recv()
    amp = amps[0, 0:1, 0:1]
    masks = plan_in[...].astype(F32)
    weight = amp * amp * masks[0:1, 0:1]
    scaled = (weight * inverse_of(s0[...])).astype(BF16)
    total = jnp.dot(scaled, cw[row], preferred_element_type=F32)
    visited(ring - 1)
    gather_sums(ring - 1)
    weight = amps[1, 0:1, 0:1] * amp * masks[0:1, 1:2]
    for side in (0, 1):

        @pl.when(even & toward[1 - side])
        def _():
            own[...] += sum_in[side]

    scaled = (weight * inverse_of(own[...])).astype(BF16)
    total = total + jnp.dot(scaled, vis[...], preferred_element_type=F32)
    folded[det] = total.astype(BF16)

    def span_of(half):
        return pl.ds(half * half_size, half_size)

    def send_folded(source, half, target, send):
        span = folded.at[source, :, span_of(half)]
        return remote(span, span, send, folded_recv.at[source, half], det=target)

    def to_pair(source, half):
        return send_folded(source, half, partner, pair_send.at[source, half])

    def landed(source, half):
        to_pair(source, half).wait_recv()

    sink = out_ref if width == rows else wide

    def piece_here(source):
        remote(
            cw.at[0, :, pl.ds(0, width)], pieces.at[source], piece_send.at[0, 0], piece_recv.at[source],
            det=partner,
        ).wait_recv()

    def add(source, half):
        sink[:, span_of(half)] += gram(pieces[source], folded[source, :, span_of(half)])

    def add_own():
        own_start = lax.rem(det, per_block) * rows // width * width
        mine = cw[det // per_block, :, pl.ds(pl.multiple_of(own_start, width), width)]
        sink[...] = gram(mine, folded[det])
        piece_here(partner)
        for half in range(n_halves):
            landed(partner, half)
            add(partner, half)

    def arrived(source, half, then=None):
        landed(source, half)
        if then is not None:
            then()
        to_pair(source, half).start()

    def foreign(source, half):
        if half == 0:
            piece_here(source)
        add(source, half)

    halves = range(n_halves)
    if chips == 4:
        across_x = chip + 1 - 2 * lax.rem(chip, 2)
        across_y = lax.rem(chip + 2, 4)
        corner = (3 - chip) * 2
        first = jnp.where(even, across_x, across_y) * 2
        second = jnp.where(even, across_y, across_x) * 2

        def near(which, half):
            target = (first if which == 0 else second) + core
            return send_folded(det, half, target, near_send.at[which, half])

        def relay(half):
            return send_folded(first + core, half, second + core, relay_send.at[half])

        for half in halves:
            near(0, half).start()
        for half in halves:
            near(1, half).start()
        for half in halves:
            to_pair(det, half).start()
        add_own()
        for half in halves:
            arrived(first + core, half, relay(half).start)
            foreign(first + core, half)
        for half in halves:
            arrived(second + core, half)
            foreign(second + core, half)
        for other in (second, first):
            for half in halves:
                landed(other + 1 - core, half)
                foreign(other + 1 - core, half)
        for half in halves:
            arrived(corner + core, half)
            foreign(corner + core, half)
        for half in halves:
            landed(corner + 1 - core, half)
            foreign(corner + 1 - core, half)
        for half in halves:
            near(0, half).wait_send()
            near(1, half).wait_send()
            relay(half).wait_send()
            for source in (det, first + core, second + core, corner + core):
                to_pair(source, half).wait_send()
    else:

        def to_chip(i, half):
            target = lax.rem(chip + 1 + i, chips) * 2 + core
            return send_folded(det, half, target, near_send.at[i, half])

        def other(i):
            return lax.rem(chip + chips - 1 - i, chips) * 2

        def relay_all(i):
            for half in halves:
                arrived(other(i) + core, half)
                foreign(other(i) + core, half)

        def relayed(i):
            for half in halves:
                landed(other(i) + 1 - core, half)
                foreign(other(i) + 1 - core, half)

        for half in halves:
            each(chips - 1, lambda i: to_chip(i, half).start())
            to_pair(det, half).start()
        add_own()
        each(chips - 1, relay_all)
        each(chips - 1, relayed)
        for half in halves:
            each(chips - 1, lambda i: to_chip(i, half).wait_send())
            to_pair(det, half).wait_send()
            each(chips - 1, lambda i: to_pair(other(i) + core, half).wait_send())
    if width != rows:
        out_ref[...] = wide[pl.ds(pl.multiple_of(lax.rem(det * rows, width), rows), rows)]

    visit.wait_send()
    visit_amp.wait_send()
    for side in (0, 1):
        for q in range(n_chunks):
            pass_on(row, side, q, wait=True)

        @pl.when(even & toward[side])
        def _():
            for k in range(len(sum_parts)):
                sum_copy(k, side).wait_send()

    for half in halves:
        hand_out(row, half, wait=True)
    for distance in range(1, ring):
        for side, block, there in blocks_at(distance):

            @pl.when(there)
            def _():
                for q in range(n_chunks):
                    pass_on(block, side, q, wait=True)
                for half in halves:
                    hand_out(block, half, wait=True)

            @pl.when(there & even)
            def _():
                for half in halves:
                    to_partner(block, half).wait_send()


def on_device(coefficients, amplitudes, plan):
    n, ring = lax.axis_size("det"), lax.axis_size("row")
    if coefficients.shape[0] != 1 or plan.shape[1] != 2:
        raise ValueError("unsupported sizes")
    block = jnp.swapaxes(coefficients, 1, 2)[0]
    orbitals, size = block.shape
    rows = size * ring // n
    width = max(rows, 128)
    chunks, halves = splits(n, ring, size)
    dma = pltpu.SemaphoreType.DMA
    lanes = -(-orbitals // 128) * 128
    used = 2 * orbitals * (size * (2 * ring + 1 + n) + width * n) + 24 * orbitals * lanes + 4 * size * (rows + width)
    return pl.pallas_call(
        functools.partial(kernel, n, ring),
        out_shape=jax.ShapeDtypeStruct((rows, size), F32),
        in_specs=[pl.BlockSpec(memory_space=pltpu.HBM)] * 3,
        out_specs=pl.BlockSpec(memory_space=pltpu.VMEM),
        scratch_shapes=[
            pltpu.VMEM((ring, orbitals, size), BF16),
            pltpu.VMEM((ring, orbitals, size), BF16),
            pltpu.VMEM((orbitals, size), BF16),
            pltpu.VMEM((2, 8, 128), F32),
            pltpu.VMEM((1, 1), amplitudes.dtype),
            pltpu.VMEM((1, 2), plan.dtype),
            pltpu.VMEM((orbitals, orbitals), F32),
            pltpu.VMEM((2, orbitals, orbitals), F32),
            pltpu.VMEM((2, orbitals, orbitals), F32),
            pltpu.VMEM((orbitals, orbitals), F32),
            pltpu.VMEM((n, orbitals, width), BF16),
            pltpu.VMEM((n, orbitals, size), BF16),
            pltpu.VMEM((width, size) if width != rows else (8, 128), F32),
            dma((3,)), dma((ring, 2, chunks)), dma((ring, chunks)), dma((ring, halves)), dma((ring, halves)),
            dma((2, 4)), dma((2, 4)), dma((2,)), dma((2,)), dma((ring, n // ring)), dma((n,)),
            dma((n // 2, halves)), dma((halves,)), dma((n, halves)), dma((n, halves)),
        ],
        compiler_params=pltpu.CompilerParams(
            collective_id=0, has_side_effects=True, vmem_limit_bytes=used + 4 * 1024 * 1024
        ),
    )(block, amplitudes.reshape(1, 1), jnp.swapaxes(plan, 1, 2).reshape(1, 2))


def solution(mesh):
    placed = (P("det", "row", None), P("det"), P("det", None, None))
    return jax.shard_map(
        on_device, mesh=mesh, in_specs=placed, out_specs=P("det", "row"), check_vma=False
    )
```

```python
import functools

import jax
import jax.numpy as jnp
from jax import lax
from jax.experimental import pallas as pl
from jax.experimental.pallas import tpu as pltpu
from jax.sharding import PartitionSpec as P

ORDER = 2
F32 = jnp.float32
BF16 = jnp.bfloat16


def each(count, body):
    if count <= 8:
        for i in range(count):
            body(i)
    else:
        lax.fori_loop(0, count, lambda i, c: (body(i), c)[1], 0)


def inverse_of(correlation):
    size = correlation.shape[0]
    row = lax.broadcasted_iota(jnp.int32, (size, size), 0)
    col = lax.broadcasted_iota(jnp.int32, (size, size), 1)
    identity = jnp.where(row == col, 1.0, 0.0).astype(F32)
    remainder = identity - correlation
    inverse = identity + remainder
    for level in range(ORDER - 1):
        inverse = identity + jnp.dot(
            remainder, inverse, precision=lax.Precision.HIGHEST, preferred_element_type=F32
        )
    return inverse


def gram(a, b):
    return lax.dot_general(a, b, (((0,), (0,)), ((), ())), preferred_element_type=F32)


def against(a, b):
    return lax.dot_general(a, b, (((1,), (1,)), ((), ())), preferred_element_type=F32)


def parts_of(size, count):
    step = -(-size // (8 * count)) * 8
    return [(start, min(step, size - start)) for start in range(0, size, step)]


def splits(n, ring, size):
    halves = 2 if (n // ring) % 2 == 0 and size % 256 == 0 else 1
    chunks = 2 * halves if size % (256 * halves) == 0 else halves
    return chunks, halves


def kernel(
    n, ring, c_ref, amp_ref, plan_ref, out_ref,
    cw, vw, vis, amps, amp_in, plan_in, own, sum_in, sum_out, s0, pieces, folded, wide,
    local_sem, cw_send, cw_recv, vw_send, vw_recv, sum_send, sum_recv, vis_send, vis_recv,
    piece_send, piece_recv, near_send, relay_send, pair_send, folded_recv,
):
    det = lax.axis_index("det")
    row = lax.axis_index("row")
    rows, size = out_ref.shape
    width = pieces.shape[2]
    per_block = n // ring
    chips = n // 2
    chip, core = det // 2, lax.rem(det, 2)
    partner = chip * 2 + (1 - core)
    even = core == 0
    toward = (row < ring - 1, row > 0)
    sum_parts = parts_of(own.shape[0], 4)
    n_chunks, n_halves = splits(n, ring, size)
    chunk, half_size = size // n_chunks, size // n_halves

    def remote(src, dst, send, recv, **where):
        return pltpu.make_async_remote_copy(
            src_ref=src, dst_ref=dst, send_sem=send, recv_sem=recv,
            device_id=where, device_id_type=pl.DeviceIdType.MESH,
        )

    stage = [
        pltpu.make_async_copy(c_ref, cw.at[row], local_sem.at[0]),
        pltpu.make_async_copy(amp_ref, amp_in, local_sem.at[1]),
        pltpu.make_async_copy(plan_ref, plan_in, local_sem.at[2]),
    ]
    for copy in stage:
        copy.start()

    barrier = pltpu.get_barrier_semaphore()

    def greet(i):
        peer = lax.rem(det + 1 + i, n)
        pl.semaphore_signal(barrier, inc=1, device_id={"det": peer}, device_id_type=pl.DeviceIdType.MESH)

    each(n - 1, greet)

    for side in (0, 1):

        @pl.when(toward[side])
        def _():
            peer = row + 1 - 2 * side
            pl.semaphore_signal(barrier, inc=1, device_id={"row": peer}, device_id_type=pl.DeviceIdType.MESH)

    for copy in stage:
        copy.wait()
    amps[0] = jnp.broadcast_to(amp_in[...].astype(F32), amps.shape[1:])
    s0[...] = against(cw[row], cw[row])
    pl.semaphore_wait(barrier, n - 1 + toward[0].astype(jnp.int32) + toward[1].astype(jnp.int32))

    def along(block, side, q):
        span = cw.at[block, :, pl.ds(q * chunk, chunk)]
        return remote(
            span, span, cw_send.at[block, side, q], cw_recv.at[block, q], row=row + 1 - 2 * side
        )

    def pass_on(block, side, q, wait=False):
        @pl.when(toward[side])
        def _():
            copy = along(block, side, q)
            if wait:
                copy.wait_send()
            else:
                copy.start()

    def sum_copy(k, side):
        span = pl.ds(*sum_parts[k])
        return remote(
            sum_out.at[side, span], sum_in.at[side, span], sum_send.at[side, k], sum_recv.at[side, k],
            row=row + 1 - 2 * side,
        )

    def sums(side, first):
        for k, (start, length) in enumerate(sum_parts):
            span = pl.ds(start, length)
            if not first:
                sum_copy(k, side).wait_recv()

            @pl.when(toward[side])
            def _():
                if first:
                    sum_out[side, span] = own[span]
                else:
                    sum_out[side, span] = own[span] + sum_in[side, span]
                sum_copy(k, side).start()

    def gather_sums(distance):
        @pl.when(even & (row == distance))
        def _():
            sums(0, distance == 0)

        @pl.when(even & (row == ring - 1 - distance))
        def _():
            sums(1, distance == 0)

    def piece(block, k):
        target = block * per_block + k
        start = pl.multiple_of(k * rows // width * width, width)
        return target, remote(
            cw.at[block, :, pl.ds(start, width)], pieces.at[det],
            piece_send.at[block, k], piece_recv.at[det], det=target,
        )

    def hand_out(block, half, wait=False):
        share = per_block // n_halves

        def one(i):
            target, copy = piece(block, half * share + i)

            @pl.when(target != det)
            def _():
                if wait:
                    copy.wait_send()
                else:
                    copy.start()

        each(share, one)

    def columns(ref, block, half):
        return ref[block, :, pl.ds(half * half_size, half_size)]

    def to_partner(block, half):
        span = pl.ds(half * half_size, half_size)
        return remote(
            cw.at[block, :, span], vw.at[block, :, span], vw_send.at[block, half], vw_recv.at[block, half],
            det=partner,
        )

    following = lax.rem(det + 1, n)
    visit = remote(cw.at[row], vis, vis_send.at[0], vis_recv.at[0], det=following)
    visit_amp = remote(amps.at[0], amps.at[1], vis_send.at[1], vis_recv.at[1], det=following)
    visit.start()
    visit_amp.start()
    for q in range(n_chunks):
        for side in (0, 1):
            pass_on(row, side, q)
    for half in range(n_halves):
        hand_out(row, half)
    visit.wait_recv()
    own[...] = against(vis[...], cw[row])
    gather_sums(0)

    def blocks_at(distance):
        for side in (0, 1):
            block = row - distance if side == 0 else row + distance
            yield side, block, (block >= 0) & (block < ring)

    def arrive(distance):
        for q in range(n_chunks):
            for side, block, there in blocks_at(distance):

                @pl.when(there)
                def _():
                    along(block, side, q).wait_recv()
                    pass_on(block, side, q)
                    if (q + 1) % (n_chunks // n_halves) == 0:
                        half = q // (n_chunks // n_halves)

                        @pl.when(even)
                        def _():
                            to_partner(block, half).start()

                        hand_out(block, half)
                        part = columns(cw, block, half)
                        s0[...] += against(part, part)

    def visited(distance):
        for half in range(n_halves):
            for side, block, there in blocks_at(distance):

                @pl.when(there & jnp.logical_not(even))
                def _():
                    to_partner(block, half).wait_recv()
                    own[...] += against(columns(vw, block, half), columns(cw, block, half))

    for distance in range(1, ring):
        arrive(distance)
        if distance < ring - 1:
            visited(distance)
            gather_sums(distance)
    visit_amp.wait_recv()
    amp = amps[0, 0:1, 0:1]
    masks = plan_in[...].astype(F32)
    weight = amp * amp * masks[0:1, 0:1]
    scaled = (weight * inverse_of(s0[...])).astype(BF16)
    total = jnp.dot(scaled, cw[row], preferred_element_type=F32)
    visited(ring - 1)
    gather_sums(ring - 1)
    weight = amps[1, 0:1, 0:1] * amp * masks[0:1, 1:2]
    for side in (0, 1):

        @pl.when(even & toward[1 - side])
        def _():
            own[...] += sum_in[side]

    scaled = (weight * inverse_of(own[...])).astype(BF16)
    total = total + jnp.dot(scaled, vis[...], preferred_element_type=F32)
    folded[det] = total.astype(BF16)

    def span_of(half):
        return pl.ds(half * half_size, half_size)

    def send_folded(source, half, target, send):
        span = folded.at[source, :, span_of(half)]
        return remote(span, span, send, folded_recv.at[source, half], det=target)

    def to_pair(source, half):
        return send_folded(source, half, partner, pair_send.at[source, half])

    def landed(source, half):
        to_pair(source, half).wait_recv()

    sink = out_ref if width == rows else wide

    def piece_here(source):
        remote(
            cw.at[0, :, pl.ds(0, width)], pieces.at[source], piece_send.at[0, 0], piece_recv.at[source],
            det=partner,
        ).wait_recv()

    def add(source, half):
        sink[:, span_of(half)] += gram(pieces[source], folded[source, :, span_of(half)])

    def add_own():
        own_start = lax.rem(det, per_block) * rows // width * width
        mine = cw[det // per_block, :, pl.ds(pl.multiple_of(own_start, width), width)]
        sink[...] = gram(mine, folded[det])
        piece_here(partner)
        for half in range(n_halves):
            landed(partner, half)
            add(partner, half)

    def arrived(source, half, then=None):
        landed(source, half)
        if then is not None:
            then()
        to_pair(source, half).start()

    def foreign(source, half):
        if half == 0:
            piece_here(source)
        add(source, half)

    halves = range(n_halves)
    if chips == 4:
        across_x = chip + 1 - 2 * lax.rem(chip, 2)
        across_y = lax.rem(chip + 2, 4)
        corner = (3 - chip) * 2
        first = jnp.where(even, across_x, across_y) * 2
        second = jnp.where(even, across_y, across_x) * 2

        def near(which, half):
            target = (first if which == 0 else second) + core
            return send_folded(det, half, target, near_send.at[which, half])

        def relay(half):
            return send_folded(first + core, half, second + core, relay_send.at[half])

        for half in halves:
            near(0, half).start()
        for half in halves:
            near(1, half).start()
        for half in halves:
            to_pair(det, half).start()
        add_own()
        for half in halves:
            arrived(first + core, half, relay(half).start)
            foreign(first + core, half)
        for half in halves:
            arrived(second + core, half)
            foreign(second + core, half)
        for other in (second, first):
            for half in halves:
                landed(other + 1 - core, half)
                foreign(other + 1 - core, half)
        for half in halves:
            arrived(corner + core, half)
            foreign(corner + core, half)
        for half in halves:
            landed(corner + 1 - core, half)
            foreign(corner + 1 - core, half)
        for half in halves:
            near(0, half).wait_send()
            near(1, half).wait_send()
            relay(half).wait_send()
            for source in (det, first + core, second + core, corner + core):
                to_pair(source, half).wait_send()
    else:

        def to_chip(i, half):
            target = lax.rem(chip + 1 + i, chips) * 2 + core
            return send_folded(det, half, target, near_send.at[i, half])

        def other(i):
            return lax.rem(chip + chips - 1 - i, chips) * 2

        def relay_all(i):
            for half in halves:
                arrived(other(i) + core, half)
                foreign(other(i) + core, half)

        def relayed(i):
            for half in halves:
                landed(other(i) + 1 - core, half)
                foreign(other(i) + 1 - core, half)

        for half in halves:
            each(chips - 1, lambda i: to_chip(i, half).start())
            to_pair(det, half).start()
        add_own()
        each(chips - 1, relay_all)
        each(chips - 1, relayed)
        for half in halves:
            each(chips - 1, lambda i: to_chip(i, half).wait_send())
            to_pair(det, half).wait_send()
            each(chips - 1, lambda i: to_pair(other(i) + core, half).wait_send())
    if width != rows:
        out_ref[...] = wide[pl.ds(pl.multiple_of(lax.rem(det * rows, width), rows), rows)]

    visit.wait_send()
    visit_amp.wait_send()
    for side in (0, 1):
        for q in range(n_chunks):
            pass_on(row, side, q, wait=True)

        @pl.when(even & toward[side])
        def _():
            for k in range(len(sum_parts)):
                sum_copy(k, side).wait_send()

    for half in halves:
        hand_out(row, half, wait=True)
    for distance in range(1, ring):
        for side, block, there in blocks_at(distance):

            @pl.when(there)
            def _():
                for q in range(n_chunks):
                    pass_on(block, side, q, wait=True)
                for half in halves:
                    hand_out(block, half, wait=True)

            @pl.when(there & even)
            def _():
                for half in halves:
                    to_partner(block, half).wait_send()


def on_device(coefficients, amplitudes, plan):
    n, ring = lax.axis_size("det"), lax.axis_size("row")
    if coefficients.shape[0] != 1 or plan.shape[1] != 2:
        raise ValueError("unsupported sizes")
    block = jnp.swapaxes(coefficients, 1, 2)[0]
    orbitals, size = block.shape
    rows = size * ring // n
    width = max(rows, 128)
    chunks, halves = splits(n, ring, size)
    dma = pltpu.SemaphoreType.DMA
    lanes = -(-orbitals // 128) * 128
    used = 2 * orbitals * (size * (2 * ring + 1 + n) + width * n) + 24 * orbitals * lanes + 4 * size * (rows + width)
    return pl.pallas_call(
        functools.partial(kernel, n, ring),
        out_shape=jax.ShapeDtypeStruct((rows, size), F32),
        in_specs=[pl.BlockSpec(memory_space=pltpu.HBM)] * 3,
        out_specs=pl.BlockSpec(memory_space=pltpu.VMEM),
        scratch_shapes=[
            pltpu.VMEM((ring, orbitals, size), BF16),
            pltpu.VMEM((ring, orbitals, size), BF16),
            pltpu.VMEM((orbitals, size), BF16),
            pltpu.VMEM((2, 8, 128), F32),
            pltpu.VMEM((1, 1), amplitudes.dtype),
            pltpu.VMEM((1, 2), plan.dtype),
            pltpu.VMEM((orbitals, orbitals), F32),
            pltpu.VMEM((2, orbitals, orbitals), F32),
            pltpu.VMEM((2, orbitals, orbitals), F32),
            pltpu.VMEM((orbitals, orbitals), F32),
            pltpu.VMEM((n, orbitals, width), BF16),
            pltpu.VMEM((n, orbitals, size), BF16),
            pltpu.VMEM((width, size) if width != rows else (8, 128), F32),
            dma((3,)), dma((ring, 2, chunks)), dma((ring, chunks)), dma((ring, halves)), dma((ring, halves)),
            dma((2, 4)), dma((2, 4)), dma((2,)), dma((2,)), dma((ring, n // ring)), dma((n,)),
            dma((n // 2, halves)), dma((halves,)), dma((n, halves)), dma((n, halves)),
        ],
        compiler_params=pltpu.CompilerParams(
            collective_id=0, has_side_effects=True, vmem_limit_bytes=used + 4 * 1024 * 1024
        ),
    )(
        pltpu.with_memory_space_constraint(block, pltpu.HBM),
        amplitudes.reshape(1, 1),
        pltpu.with_memory_space_constraint(jnp.swapaxes(plan, 1, 2).reshape(1, 2), pltpu.HBM),
    )


def solution(mesh):
    placed = (P("det", "row", None), P("det"), P("det", None, None))
    return jax.shard_map(
        on_device, mesh=mesh, in_specs=placed, out_specs=P("det", "row"), check_vma=False
    )
```

```python
import functools

import jax
import jax.numpy as jnp
from jax import lax
from jax.experimental import pallas as pl
from jax.experimental.pallas import tpu as pltpu
from jax.sharding import PartitionSpec as P

ORDER = 2
F32 = jnp.float32
BF16 = jnp.bfloat16


def each(count, body):
    if count <= 8:
        for i in range(count):
            body(i)
    else:
        lax.fori_loop(0, count, lambda i, c: (body(i), c)[1], 0)


def inverse_of(correlation):
    size = correlation.shape[0]
    row = lax.broadcasted_iota(jnp.int32, (size, size), 0)
    col = lax.broadcasted_iota(jnp.int32, (size, size), 1)
    identity = jnp.where(row == col, 1.0, 0.0).astype(F32)
    remainder = identity - correlation
    inverse = identity + remainder
    for level in range(ORDER - 1):
        inverse = identity + jnp.dot(
            remainder, inverse, precision=lax.Precision.HIGHEST, preferred_element_type=F32
        )
    return inverse


def gram(a, b):
    return lax.dot_general(a, b, (((0,), (0,)), ((), ())), preferred_element_type=F32)


def against(a, b):
    return lax.dot_general(a, b, (((1,), (1,)), ((), ())), preferred_element_type=F32)


def parts_of(size, count):
    step = -(-size // (8 * count)) * 8
    return [(start, min(step, size - start)) for start in range(0, size, step)]


def splits(n, ring, size):
    halves = 2 if (n // ring) % 2 == 0 and size % 256 == 0 else 1
    chunks = 2 * halves if size % (256 * halves) == 0 else halves
    return chunks, halves


def kernel(
    n, ring, c_ref, amp_ref, plan_ref, out_ref,
    cw, vw, vis, scaled, amps, amp_in, plan_in, own, sum_in, sum_out, s0, pieces, folded, wide,
    local_sem, cw_send, cw_recv, vw_send, vw_recv, sum_send, sum_recv, vis_send, vis_recv,
    piece_send, piece_recv, throw_send, serve_send, serve_recv, near_send, relay_send, pair_send, folded_recv,
):
    det = lax.axis_index("det")
    row = lax.axis_index("row")
    rows, size = out_ref.shape
    width = pieces.shape[2]
    per_block = n // ring
    chips = n // 2
    chip, core = det // 2, lax.rem(det, 2)
    partner = chip * 2 + (1 - core)
    even = core == 0
    quad = chips == 4 and per_block == 2
    home, corner = det // per_block, chips - 1 - chip
    served = ring >= 4
    reach = ring - 2 if served else ring - 1
    at_end = (row == 0) | (row == ring - 1)
    serves = even & ((row == 1) | (row == ring - 2))
    throws = (row == home) & ((row == 0) | (row == ring - 1))
    toward = (row < ring - 1, row > 0)
    sum_parts = parts_of(own.shape[0], 4)
    n_chunks, n_halves = splits(n, ring, size)
    chunk, half_size = size // n_chunks, size // n_halves

    def remote(src, dst, send, recv, **where):
        return pltpu.make_async_remote_copy(
            src_ref=src, dst_ref=dst, send_sem=send, recv_sem=recv,
            device_id=where, device_id_type=pl.DeviceIdType.MESH,
        )

    stage = [
        pltpu.make_async_copy(c_ref, cw.at[row], local_sem.at[0]),
        pltpu.make_async_copy(amp_ref, amp_in, local_sem.at[1]),
        pltpu.make_async_copy(plan_ref, plan_in, local_sem.at[2]),
    ]
    for copy in stage:
        copy.start()

    barrier = pltpu.get_barrier_semaphore()

    def greet(i):
        peer = lax.rem(det + 1 + i, n)
        pl.semaphore_signal(barrier, inc=1, device_id={"det": peer}, device_id_type=pl.DeviceIdType.MESH)

    each(n - 1, greet)

    for side in (0, 1):

        @pl.when(toward[side])
        def _():
            peer = row + 1 - 2 * side
            pl.semaphore_signal(barrier, inc=1, device_id={"row": peer}, device_id_type=pl.DeviceIdType.MESH)

    for copy in stage:
        copy.wait()
    amps[0] = jnp.broadcast_to(amp_in[...].astype(F32), amps.shape[1:])
    s0[...] = against(cw[row], cw[row])
    pl.semaphore_wait(barrier, n - 1 + toward[0].astype(jnp.int32) + toward[1].astype(jnp.int32))

    def along(block, side, q):
        span = cw.at[block, :, pl.ds(q * chunk, chunk)]
        return remote(
            span, span, cw_send.at[block, side, q], cw_recv.at[block, q], row=row + 1 - 2 * side
        )

    def pass_on(block, side, q, wait=False):
        @pl.when(toward[side])
        def _():
            copy = along(block, side, q)
            if wait:
                copy.wait_send()
            else:
                copy.start()

    def sum_copy(k, side):
        span = pl.ds(*sum_parts[k])
        return remote(
            sum_out.at[side, span], sum_in.at[side, span], sum_send.at[side, k], sum_recv.at[side, k],
            row=row + 1 - 2 * side,
        )

    def sums(side, distance):
        for k, (start, length) in enumerate(sum_parts):
            span = pl.ds(start, length)
            if distance:
                sum_copy(k, side).wait_recv()
            if distance < reach:
                sum_out[side, span] = own[span] + sum_in[side, span] if distance else own[span]
                sum_copy(k, side).start()

    def gather_sums(distance):
        if distance > reach:
            return

        @pl.when(even & (row == distance))
        def _():
            sums(0, distance)

        @pl.when(even & (row == ring - 1 - distance))
        def _():
            sums(1, distance)

    def piece(block, k):
        target = block * per_block + k
        start = pl.multiple_of(k * rows // width * width, width)
        return target, remote(
            cw.at[block, :, pl.ds(start, width)], pieces.at[det],
            piece_send.at[block, k], piece_recv.at[det], det=target,
        )

    def hand_out(block, half, wait=False):
        share = per_block // n_halves

        def one(i):
            target, copy = piece(block, half * share + i)

            direct = target != det
            if quad:
                direct &= (jnp.abs(block - row) < ring - 1) | (corner != block)

            @pl.when(direct)
            def _():
                if wait:
                    copy.wait_send()
                else:
                    copy.start()

        each(share, one)

    def thrown(i, wait=False):
        source = corner * 2 + i
        copy = remote(
            pieces.at[source], pieces.at[source], throw_send.at[i], piece_recv.at[source],
            row=ring - 1 - row,
        )

        @pl.when(throws)
        def _():
            if wait:
                copy.wait_send()
            else:
                copy.wait_recv()
                copy.start()

    def columns(ref, block, half):
        return ref[block, :, pl.ds(half * half_size, half_size)]

    def to_partner(block, half):
        span = pl.ds(half * half_size, half_size)
        return remote(
            cw.at[block, :, span], vw.at[block, :, span], vw_send.at[block, half], vw_recv.at[block, half],
            det=partner,
        )

    following = lax.rem(det + 1, n)
    visit = remote(cw.at[row], vis, vis_send.at[0], vis_recv.at[0], det=following)
    visit_amp = remote(amps.at[0], amps.at[1], vis_send.at[1], vis_recv.at[1], det=following)
    visit.start()
    visit_amp.start()
    for q in range(n_chunks):
        for side in (0, 1):
            pass_on(row, side, q)
    visit.wait_recv()
    own[...] = against(vis[...], cw[row])
    gather_sums(0)
    for half in range(n_halves):
        hand_out(row, half)

    def blocks_at(distance):
        for side in (0, 1):
            block = row - distance if side == 0 else row + distance
            yield side, block, (block >= 0) & (block < ring)

    def arrive(distance):
        for q in range(n_chunks):
            for side, block, there in blocks_at(distance):

                @pl.when(there)
                def _():
                    along(block, side, q).wait_recv()
                    pass_on(block, side, q)
                    if (q + 1) % (n_chunks // n_halves) == 0:
                        half = q // (n_chunks // n_halves)

                        @pl.when(even)
                        def _():
                            to_partner(block, half).start()

                        hand_out(block, half)
                        part = columns(cw, block, half)
                        s0[...] += against(part, part)

    def visited(distance):
        for half in range(n_halves):
            for side, block, there in blocks_at(distance):

                @pl.when(there & jnp.logical_not(even))
                def _():
                    to_partner(block, half).wait_recv()
                    own[...] += against(columns(vw, block, half), columns(cw, block, half))

    for distance in range(1, ring):
        arrive(distance)
        if distance < ring - 1:
            visited(distance)
            gather_sums(distance)
    visit_amp.wait_recv()
    amp = amps[0, 0:1, 0:1]
    masks = plan_in[...].astype(F32)
    is_served = even & at_end if served else jnp.bool_(False)
    serve = remote(scaled.at[1], scaled.at[1], serve_send, serve_recv, row=jnp.where(row == 1, 0, ring - 1))

    def scale_visitor():
        for side in (0, 1):

            @pl.when(even & toward[1 - side])
            def _():
                own[...] += sum_in[side]

        weight = amps[1, 0:1, 0:1] * amp * masks[0:1, 1:2]
        scaled[1] = (weight * inverse_of(own[...])).astype(BF16)

    if served:

        @pl.when(serves)
        def _():
            scale_visitor()
            serve.start()

    weight = amp * amp * masks[0:1, 0:1]
    scaled[0] = (weight * inverse_of(s0[...])).astype(BF16)
    total = jnp.dot(scaled[0], cw[row], preferred_element_type=F32)
    visited(ring - 1)
    gather_sums(ring - 1)
    pl.when(jnp.logical_not(is_served | serves) if served else jnp.bool_(True))(scale_visitor)
    if served:
        pl.when(is_served)(serve.wait_recv)
    total = total + jnp.dot(scaled[1], vis[...], preferred_element_type=F32)
    folded[det] = total.astype(BF16)

    def span_of(half):
        return pl.ds(half * half_size, half_size)

    def send_folded(source, half, target, send):
        span = folded.at[source, :, span_of(half)]
        return remote(span, span, send, folded_recv.at[source, half], det=target)

    def to_pair(source, half):
        return send_folded(source, half, partner, pair_send.at[source, half])

    def landed(source, half):
        to_pair(source, half).wait_recv()

    sink = out_ref if width == rows else wide

    def piece_here(source):
        remote(
            cw.at[0, :, pl.ds(0, width)], pieces.at[source], piece_send.at[0, 0], piece_recv.at[source],
            det=partner,
        ).wait_recv()

    def add(source, half):
        sink[:, span_of(half)] += gram(pieces[source], folded[source, :, span_of(half)])

    def add_own():
        own_start = lax.rem(det, per_block) * rows // width * width
        mine = cw[det // per_block, :, pl.ds(pl.multiple_of(own_start, width), width)]
        sink[...] = gram(mine, folded[det])
        piece_here(partner)
        for half in range(n_halves):
            landed(partner, half)
            add(partner, half)

    def arrived(source, half, then=None):
        landed(source, half)
        if then is not None:
            then()
        to_pair(source, half).start()

    def foreign(source, half, detoured=False):
        if half == 0:

            @pl.when(jnp.logical_not(detoured & throws))
            def _():
                piece_here(source)

        add(source, half)

    halves = range(n_halves)
    if quad:
        across_x = chip + 1 - 2 * lax.rem(chip, 2)
        across_y = lax.rem(chip + 2, 4)
        far = corner * 2
        first = jnp.where(even, across_x, across_y) * 2
        second = jnp.where(even, across_y, across_x) * 2

        def near(which, half):
            target = (first if which == 0 else second) + core
            return send_folded(det, half, target, near_send.at[which, half])

        def relay(half):
            return send_folded(first + core, half, second + core, relay_send.at[half])

        def across(half):
            return send_folded(det, half, far + core, relay_send.at[half])

        for half in halves:
            near(0, half).start()
        for half in halves:
            to_pair(det, half).start()
        add_own()
        for half in halves:
            near(1, half).start()
        thrown(0)
        thrown(1)
        for half in halves:
            arrived(first + core, half, relay(half).start)
        for half in halves:
            foreign(first + core, half)
        for half in halves:
            arrived(second + core, half)
        for half in halves:
            foreign(second + core, half)
        for other in (second, first):
            for half in halves:
                landed(other + 1 - core, half)
                foreign(other + 1 - core, half)
        for half in halves:
            arrived(far + core, half)
            foreign(far + core, half, True)
        for half in halves:
            landed(far + 1 - core, half)
            foreign(far + 1 - core, half, True)
        for half in halves:
            near(0, half).wait_send()
            near(1, half).wait_send()
            relay(half).wait_send()
            for source in (det, first + core, second + core, far + core):
                to_pair(source, half).wait_send()
        thrown(0, wait=True)
        thrown(1, wait=True)
    else:

        def to_chip(i, half):
            target = lax.rem(chip + 1 + i, chips) * 2 + core
            return send_folded(det, half, target, near_send.at[i, half])

        def other(i):
            return lax.rem(chip + chips - 1 - i, chips) * 2

        def relay_all(i):
            for half in halves:
                arrived(other(i) + core, half)
                foreign(other(i) + core, half)

        def relayed(i):
            for half in halves:
                landed(other(i) + 1 - core, half)
                foreign(other(i) + 1 - core, half)

        for half in halves:
            each(chips - 1, lambda i: to_chip(i, half).start())
            to_pair(det, half).start()
        add_own()
        each(chips - 1, relay_all)
        each(chips - 1, relayed)
        for half in halves:
            each(chips - 1, lambda i: to_chip(i, half).wait_send())
            to_pair(det, half).wait_send()
            each(chips - 1, lambda i: to_pair(other(i) + core, half).wait_send())
    if width != rows:
        out_ref[...] = wide[pl.ds(pl.multiple_of(lax.rem(det * rows, width), rows), rows)]

    if served:
        pl.when(serves)(serve.wait_send)
    visit.wait_send()
    visit_amp.wait_send()
    for side in (0, 1):
        for q in range(n_chunks):
            pass_on(row, side, q, wait=True)

        passed = row < reach if side == 0 else row > ring - 1 - reach

        @pl.when(even & passed)
        def _():
            for k in range(len(sum_parts)):
                sum_copy(k, side).wait_send()

    for half in halves:
        hand_out(row, half, wait=True)
    for distance in range(1, ring):
        for side, block, there in blocks_at(distance):

            @pl.when(there)
            def _():
                for q in range(n_chunks):
                    pass_on(block, side, q, wait=True)
                for half in halves:
                    hand_out(block, half, wait=True)

            @pl.when(there & even)
            def _():
                for half in halves:
                    to_partner(block, half).wait_send()


def on_device(coefficients, amplitudes, plan):
    n, ring = lax.axis_size("det"), lax.axis_size("row")
    if coefficients.shape[0] != 1 or plan.shape[1] != 2:
        raise ValueError("unsupported sizes")
    block = jnp.swapaxes(coefficients, 1, 2)[0]
    orbitals, size = block.shape
    rows = size * ring // n
    width = max(rows, 128)
    chunks, halves = splits(n, ring, size)
    dma = pltpu.SemaphoreType.DMA
    lanes = -(-orbitals // 128) * 128
    used = 2 * orbitals * (size * (2 * ring + 1 + n) + width * n) + 28 * orbitals * lanes + 4 * size * (rows + width)
    return pl.pallas_call(
        functools.partial(kernel, n, ring),
        out_shape=jax.ShapeDtypeStruct((rows, size), F32),
        in_specs=[pl.BlockSpec(memory_space=pltpu.HBM)] * 3,
        out_specs=pl.BlockSpec(memory_space=pltpu.VMEM),
        scratch_shapes=[
            pltpu.VMEM((ring, orbitals, size), BF16),
            pltpu.VMEM((ring, orbitals, size), BF16),
            pltpu.VMEM((orbitals, size), BF16),
            pltpu.VMEM((2, orbitals, orbitals), BF16),
            pltpu.VMEM((2, 8, 128), F32),
            pltpu.VMEM((1, 1), amplitudes.dtype),
            pltpu.VMEM((1, 2), plan.dtype),
            pltpu.VMEM((orbitals, orbitals), F32),
            pltpu.VMEM((2, orbitals, orbitals), F32),
            pltpu.VMEM((2, orbitals, orbitals), F32),
            pltpu.VMEM((orbitals, orbitals), F32),
            pltpu.VMEM((n, orbitals, width), BF16),
            pltpu.VMEM((n, orbitals, size), BF16),
            pltpu.VMEM((width, size) if width != rows else (8, 128), F32),
            dma((3,)), dma((ring, 2, chunks)), dma((ring, chunks)), dma((ring, halves)), dma((ring, halves)),
            dma((2, 4)), dma((2, 4)), dma((2,)), dma((2,)), dma((ring, n // ring)), dma((n,)), dma((2,)), dma, dma,
            dma((n // 2, halves)), dma((halves,)), dma((n, halves)), dma((n, halves)),
        ],
        compiler_params=pltpu.CompilerParams(
            collective_id=0, has_side_effects=True, vmem_limit_bytes=used + 4 * 1024 * 1024
        ),
    )(
        pltpu.with_memory_space_constraint(block, pltpu.HBM),
        amplitudes.reshape(1, 1),
        pltpu.with_memory_space_constraint(jnp.swapaxes(plan, 1, 2).reshape(1, 2), pltpu.HBM),
    )


def solution(mesh):
    placed = (P("det", "row", None), P("det"), P("det", None, None))
    return jax.shard_map(
        on_device, mesh=mesh, in_specs=placed, out_specs=P("det", "row"), check_vma=False
    )
```

```python
import functools

import jax
import jax.numpy as jnp
from jax import lax
from jax.experimental import pallas as pl
from jax.experimental.pallas import tpu as pltpu
from jax.sharding import PartitionSpec as P

ORDER = 2
F32 = jnp.float32
BF16 = jnp.bfloat16


def each(count, body):
    if count <= 8:
        for i in range(count):
            body(i)
    else:
        lax.fori_loop(0, count, lambda i, c: (body(i), c)[1], 0)


def inverse_of(correlation):
    size = correlation.shape[0]
    row = lax.broadcasted_iota(jnp.int32, (size, size), 0)
    col = lax.broadcasted_iota(jnp.int32, (size, size), 1)
    identity = jnp.where(row == col, 1.0, 0.0).astype(F32)
    remainder = identity - correlation
    inverse = identity + remainder
    for level in range(ORDER - 1):
        inverse = identity + jnp.dot(
            remainder, inverse, precision=lax.Precision.HIGHEST, preferred_element_type=F32
        )
    return inverse


def gram(a, b):
    return lax.dot_general(a, b, (((0,), (0,)), ((), ())), preferred_element_type=F32)


def against(a, b):
    return lax.dot_general(a, b, (((1,), (1,)), ((), ())), preferred_element_type=F32)


def parts_of(size, count):
    step = -(-size // (8 * count)) * 8
    return [(start, min(step, size - start)) for start in range(0, size, step)]


def splits(n, ring, size):
    halves = 2 if (n // ring) % 2 == 0 and size % 256 == 0 else 1
    chunks = 2 * halves if size % (256 * halves) == 0 else halves
    return chunks, halves


def kernel(
    n, ring, c_ref, amp_ref, plan_ref, out_ref,
    cw, vw, vis, scaled, amps, amp_in, plan_in, own, sum_in, sum_out, s0, pieces, folded, wide,
    local_sem, cw_send, cw_recv, vw_send, vw_recv, sum_send, sum_recv, vis_send, vis_recv,
    piece_send, piece_recv, throw_send, serve_send, serve_recv, near_send, relay_send, pair_send, folded_recv,
):
    det = lax.axis_index("det")
    row = lax.axis_index("row")
    rows, size = out_ref.shape
    width = pieces.shape[2]
    per_block = n // ring
    chips = n // 2
    chip, core = det // 2, lax.rem(det, 2)
    partner = chip * 2 + (1 - core)
    even = core == 0
    quad = chips == 4 and per_block == 2
    home, corner = det // per_block, chips - 1 - chip
    served = ring >= 4
    reach = ring - 2 if served else ring - 1
    at_end = (row == 0) | (row == ring - 1)
    serves = even & ((row == 1) | (row == ring - 2))
    throws = (row == home) & ((row == 0) | (row == ring - 1))
    toward = (row < ring - 1, row > 0)
    sum_parts = parts_of(own.shape[0], 4)
    n_chunks, n_halves = splits(n, ring, size)
    chunk, half_size = size // n_chunks, size // n_halves

    def remote(src, dst, send, recv, **where):
        return pltpu.make_async_remote_copy(
            src_ref=src, dst_ref=dst, send_sem=send, recv_sem=recv,
            device_id=where, device_id_type=pl.DeviceIdType.MESH,
        )

    stage = [
        pltpu.make_async_copy(c_ref, cw.at[row], local_sem.at[0]),
        pltpu.make_async_copy(amp_ref, amp_in, local_sem.at[1]),
        pltpu.make_async_copy(plan_ref, plan_in, local_sem.at[2]),
    ]
    for copy in stage:
        copy.start()

    barrier = pltpu.get_barrier_semaphore()

    def greet(i):
        peer = lax.rem(det + 1 + i, n)
        pl.semaphore_signal(barrier, inc=1, device_id={"det": peer}, device_id_type=pl.DeviceIdType.MESH)

    each(n - 1, greet)

    for side in (0, 1):

        @pl.when(toward[side])
        def _():
            peer = row + 1 - 2 * side
            pl.semaphore_signal(barrier, inc=1, device_id={"row": peer}, device_id_type=pl.DeviceIdType.MESH)

    for copy in stage:
        copy.wait()
    amps[0] = jnp.broadcast_to(amp_in[...].astype(F32), amps.shape[1:])
    s0[...] = against(cw[row], cw[row])
    pl.semaphore_wait(barrier, n - 1 + toward[0].astype(jnp.int32) + toward[1].astype(jnp.int32))

    def along(block, side, q):
        span = cw.at[block, :, pl.ds(q * chunk, chunk)]
        return remote(
            span, span, cw_send.at[block, side, q], cw_recv.at[block, q], row=row + 1 - 2 * side
        )

    def pass_on(block, side, q, wait=False):
        @pl.when(toward[side])
        def _():
            copy = along(block, side, q)
            if wait:
                copy.wait_send()
            else:
                copy.start()

    def sum_copy(k, side):
        span = pl.ds(*sum_parts[k])
        return remote(
            sum_out.at[side, span], sum_in.at[side, span], sum_send.at[side, k], sum_recv.at[side, k],
            row=row + 1 - 2 * side,
        )

    def sums(side, distance):
        for k, (start, length) in enumerate(sum_parts):
            span = pl.ds(start, length)
            if distance:
                sum_copy(k, side).wait_recv()
            if distance < reach:
                sum_out[side, span] = own[span] + sum_in[side, span] if distance else own[span]
                sum_copy(k, side).start()

    def gather_sums(distance):
        if distance > reach:
            return

        @pl.when(even & (row == distance))
        def _():
            sums(0, distance)

        @pl.when(even & (row == ring - 1 - distance))
        def _():
            sums(1, distance)

    def piece(block, k):
        target = block * per_block + k
        start = pl.multiple_of(k * rows // width * width, width)
        return target, remote(
            cw.at[block, :, pl.ds(start, width)], pieces.at[det],
            piece_send.at[block, k], piece_recv.at[det], det=target,
        )

    def hand_out(block, half, wait=False):
        share = per_block // n_halves

        def one(i):
            target, copy = piece(block, half * share + i)

            direct = target != det
            if quad:
                direct &= (jnp.abs(block - row) < ring - 1) | (corner != block)

            @pl.when(direct)
            def _():
                if wait:
                    copy.wait_send()
                else:
                    copy.start()

        each(share, one)

    def thrown(i, wait=False):
        source = corner * 2 + i
        copy = remote(
            pieces.at[source], pieces.at[source], throw_send.at[i], piece_recv.at[source],
            row=ring - 1 - row,
        )

        @pl.when(throws)
        def _():
            if wait:
                copy.wait_send()
            else:
                copy.wait_recv()
                copy.start()

    def columns(ref, block, half):
        return ref[block, :, pl.ds(half * half_size, half_size)]

    def to_partner(block, half):
        span = pl.ds(half * half_size, half_size)
        return remote(
            cw.at[block, :, span], vw.at[block, :, span], vw_send.at[block, half], vw_recv.at[block, half],
            det=partner,
        )

    following = lax.rem(det + 1, n)
    visit = remote(cw.at[row], vis, vis_send.at[0], vis_recv.at[0], det=following)
    visit_amp = remote(amps.at[0], amps.at[1], vis_send.at[1], vis_recv.at[1], det=following)
    visit.start()
    visit_amp.start()
    for q in range(n_chunks):
        for side in (0, 1):
            pass_on(row, side, q)
    visit.wait_recv()
    own[...] = against(vis[...], cw[row])
    gather_sums(0)
    for half in range(n_halves):
        hand_out(row, half)

    def blocks_at(distance):
        for side in (0, 1):
            block = row - distance if side == 0 else row + distance
            yield side, block, (block >= 0) & (block < ring)

    def arrive(distance):
        for q in range(n_chunks):
            for side, block, there in blocks_at(distance):

                @pl.when(there)
                def _():
                    along(block, side, q).wait_recv()
                    pass_on(block, side, q)
                    if (q + 1) % (n_chunks // n_halves) == 0:
                        half = q // (n_chunks // n_halves)

                        @pl.when(even)
                        def _():
                            to_partner(block, half).start()

                        hand_out(block, half)
                        part = columns(cw, block, half)
                        s0[...] += against(part, part)

    def visited(distance):
        for half in range(n_halves):
            for side, block, there in blocks_at(distance):

                @pl.when(there & jnp.logical_not(even))
                def _():
                    to_partner(block, half).wait_recv()
                    own[...] += against(columns(vw, block, half), columns(cw, block, half))

    for distance in range(1, ring):
        arrive(distance)
        if distance < ring - 1:
            visited(distance)
            gather_sums(distance)
    visit_amp.wait_recv()
    amp = amps[0, 0:1, 0:1]
    masks = plan_in[...].astype(F32)
    is_served = even & at_end if served else jnp.bool_(False)
    serve = remote(scaled.at[1], scaled.at[1], serve_send, serve_recv, row=jnp.where(row == 1, 0, ring - 1))

    def scale_visitor():
        for side in (0, 1):

            @pl.when(even & toward[1 - side])
            def _():
                own[...] += sum_in[side]

        weight = amps[1, 0:1, 0:1] * amp * masks[0:1, 1:2]
        scaled[1] = (weight * inverse_of(own[...])).astype(BF16)

    if served:

        @pl.when(serves)
        def _():
            scale_visitor()
            serve.start()

    weight = amp * amp * masks[0:1, 0:1]
    scaled[0] = (weight * inverse_of(s0[...])).astype(BF16)
    total = jnp.dot(scaled[0], cw[row], preferred_element_type=F32)
    visited(ring - 1)
    gather_sums(ring - 1)
    pl.when(jnp.logical_not(is_served | serves) if served else jnp.bool_(True))(scale_visitor)
    if served:
        pl.when(is_served)(serve.wait_recv)
    total = total + jnp.dot(scaled[1], vis[...], preferred_element_type=F32)
    folded[det] = total.astype(BF16)

    def span_of(half):
        return pl.ds(half * half_size, half_size)

    def send_folded(source, half, target, send):
        span = folded.at[source, :, span_of(half)]
        return remote(span, span, send, folded_recv.at[source, half], det=target)

    def to_pair(source, half):
        return send_folded(source, half, partner, pair_send.at[source, half])

    def landed(source, half):
        to_pair(source, half).wait_recv()

    sink = out_ref if width == rows else wide

    def piece_here(source):
        remote(
            cw.at[0, :, pl.ds(0, width)], pieces.at[source], piece_send.at[0, 0], piece_recv.at[source],
            det=partner,
        ).wait_recv()

    def add(source, half):
        sink[:, span_of(half)] += gram(pieces[source], folded[source, :, span_of(half)])

    def add_own():
        own_start = lax.rem(det, per_block) * rows // width * width
        mine = cw[det // per_block, :, pl.ds(pl.multiple_of(own_start, width), width)]
        sink[...] = gram(mine, folded[det])
        piece_here(partner)
        for half in range(n_halves):
            landed(partner, half)
            add(partner, half)

    def arrived(source, half, then=None):
        landed(source, half)
        if then is not None:
            then()
        to_pair(source, half).start()

    def foreign(source, half, detoured=False):
        if half == 0:

            @pl.when(jnp.logical_not(detoured & throws))
            def _():
                piece_here(source)

        add(source, half)

    halves = range(n_halves)
    if quad:
        across_x = chip + 1 - 2 * lax.rem(chip, 2)
        across_y = lax.rem(chip + 2, 4)
        far = corner * 2
        first = jnp.where(even, across_x, across_y) * 2
        second = jnp.where(even, across_y, across_x) * 2

        def near(which, half):
            target = (first if which == 0 else second) + core
            return send_folded(det, half, target, near_send.at[which, half])

        def relay(half):
            return send_folded(first + core, half, second + core, relay_send.at[half])

        def across(half):
            return send_folded(det, half, far + core, relay_send.at[half])

        for half in halves:
            near(0, half).start()
        for half in halves:
            to_pair(det, half).start()
        add_own()
        for half in halves:
            near(1, half).start()
        thrown(0)
        thrown(1)
        for half in halves:
            arrived(first + core, half, relay(half).start)
        for half in halves:
            foreign(first + core, half)
        for half in halves:
            arrived(second + core, half)
        for half in halves:
            foreign(second + core, half)
        for other in (second, first):
            for half in halves:
                landed(other + 1 - core, half)
                foreign(other + 1 - core, half)
        for i in (0, 1):

            @pl.when(jnp.logical_not(throws))
            def _():
                piece_here(far + i)

        for half in halves:
            arrived(far + core, half)
        both = pieces[pl.ds(far, 2)].reshape(-1, width)
        for half in halves:
            landed(far + 1 - core, half)
            part = folded[pl.ds(far, 2), :, span_of(half)].reshape(-1, half_size)
            sink[:, span_of(half)] += gram(both, part)
        for half in halves:
            near(0, half).wait_send()
            near(1, half).wait_send()
            relay(half).wait_send()
            for source in (det, first + core, second + core, far + core):
                to_pair(source, half).wait_send()
        thrown(0, wait=True)
        thrown(1, wait=True)
    else:

        def to_chip(i, half):
            target = lax.rem(chip + 1 + i, chips) * 2 + core
            return send_folded(det, half, target, near_send.at[i, half])

        def other(i):
            return lax.rem(chip + chips - 1 - i, chips) * 2

        def relay_all(i):
            for half in halves:
                arrived(other(i) + core, half)
                foreign(other(i) + core, half)

        def relayed(i):
            for half in halves:
                landed(other(i) + 1 - core, half)
                foreign(other(i) + 1 - core, half)

        for half in halves:
            each(chips - 1, lambda i: to_chip(i, half).start())
            to_pair(det, half).start()
        add_own()
        each(chips - 1, relay_all)
        each(chips - 1, relayed)
        for half in halves:
            each(chips - 1, lambda i: to_chip(i, half).wait_send())
            to_pair(det, half).wait_send()
            each(chips - 1, lambda i: to_pair(other(i) + core, half).wait_send())
    if width != rows:
        out_ref[...] = wide[pl.ds(pl.multiple_of(lax.rem(det * rows, width), rows), rows)]

    if served:
        pl.when(serves)(serve.wait_send)
    visit.wait_send()
    visit_amp.wait_send()
    for side in (0, 1):
        for q in range(n_chunks):
            pass_on(row, side, q, wait=True)

        passed = row < reach if side == 0 else row > ring - 1 - reach

        @pl.when(even & passed)
        def _():
            for k in range(len(sum_parts)):
                sum_copy(k, side).wait_send()

    for half in halves:
        hand_out(row, half, wait=True)
    for distance in range(1, ring):
        for side, block, there in blocks_at(distance):

            @pl.when(there)
            def _():
                for q in range(n_chunks):
                    pass_on(block, side, q, wait=True)
                for half in halves:
                    hand_out(block, half, wait=True)

            @pl.when(there & even)
            def _():
                for half in halves:
                    to_partner(block, half).wait_send()


def on_device(coefficients, amplitudes, plan):
    n, ring = lax.axis_size("det"), lax.axis_size("row")
    if coefficients.shape[0] != 1 or plan.shape[1] != 2:
        raise ValueError("unsupported sizes")
    block = jnp.swapaxes(coefficients, 1, 2)[0]
    orbitals, size = block.shape
    rows = size * ring // n
    width = max(rows, 128)
    chunks, halves = splits(n, ring, size)
    dma = pltpu.SemaphoreType.DMA
    lanes = -(-orbitals // 128) * 128
    used = 2 * orbitals * (size * (2 * ring + 1 + n) + width * n) + 28 * orbitals * lanes + 4 * size * (rows + width)
    return pl.pallas_call(
        functools.partial(kernel, n, ring),
        out_shape=jax.ShapeDtypeStruct((rows, size), F32),
        in_specs=[pl.BlockSpec(memory_space=pltpu.HBM)] * 3,
        out_specs=pl.BlockSpec(memory_space=pltpu.VMEM),
        scratch_shapes=[
            pltpu.VMEM((ring, orbitals, size), BF16),
            pltpu.VMEM((ring, orbitals, size), BF16),
            pltpu.VMEM((orbitals, size), BF16),
            pltpu.VMEM((2, orbitals, orbitals), BF16),
            pltpu.VMEM((2, 8, 128), F32),
            pltpu.VMEM((1, 1), amplitudes.dtype),
            pltpu.VMEM((1, 2), plan.dtype),
            pltpu.VMEM((orbitals, orbitals), F32),
            pltpu.VMEM((2, orbitals, orbitals), F32),
            pltpu.VMEM((2, orbitals, orbitals), F32),
            pltpu.VMEM((orbitals, orbitals), F32),
            pltpu.VMEM((n, orbitals, width), BF16),
            pltpu.VMEM((n, orbitals, size), BF16),
            pltpu.VMEM((width, size) if width != rows else (8, 128), F32),
            dma((3,)), dma((ring, 2, chunks)), dma((ring, chunks)), dma((ring, halves)), dma((ring, halves)),
            dma((2, 4)), dma((2, 4)), dma((2,)), dma((2,)), dma((ring, n // ring)), dma((n,)), dma((2,)), dma, dma,
            dma((n // 2, halves)), dma((halves,)), dma((n, halves)), dma((n, halves)),
        ],
        compiler_params=pltpu.CompilerParams(
            collective_id=0, has_side_effects=True, vmem_limit_bytes=used + 4 * 1024 * 1024
        ),
    )(
        pltpu.with_memory_space_constraint(block, pltpu.HBM),
        amplitudes.reshape(1, 1),
        pltpu.with_memory_space_constraint(jnp.swapaxes(plan, 1, 2).reshape(1, 2), pltpu.HBM),
    )


def solution(mesh):
    placed = (P("det", "row", None), P("det"), P("det", None, None))
    return jax.shard_map(
        on_device, mesh=mesh, in_specs=placed, out_specs=P("det", "row"), check_vma=False
    )
```

```python
import functools

import jax
import jax.numpy as jnp
from jax import lax
from jax.experimental import pallas as pl
from jax.experimental.pallas import tpu as pltpu
from jax.sharding import PartitionSpec as P

ORDER = 2
F32 = jnp.float32
BF16 = jnp.bfloat16


def each(count, body):
    if count <= 8:
        for i in range(count):
            body(i)
    else:
        lax.fori_loop(0, count, lambda i, c: (body(i), c)[1], 0)


def inverse_of(correlation):
    size = correlation.shape[0]
    row = lax.broadcasted_iota(jnp.int32, (size, size), 0)
    col = lax.broadcasted_iota(jnp.int32, (size, size), 1)
    identity = jnp.where(row == col, 1.0, 0.0).astype(F32)
    remainder = identity - correlation
    inverse = identity + remainder
    for level in range(ORDER - 1):
        inverse = identity + jnp.dot(
            remainder, inverse, precision=lax.Precision.HIGHEST, preferred_element_type=F32
        )
    return inverse


def gram(a, b):
    return lax.dot_general(a, b, (((0,), (0,)), ((), ())), preferred_element_type=F32)


def against(a, b):
    return lax.dot_general(a, b, (((1,), (1,)), ((), ())), preferred_element_type=F32)


def parts_of(size, count):
    step = -(-size // (8 * count)) * 8
    return [(start, min(step, size - start)) for start in range(0, size, step)]


def splits(n, ring, size):
    halves = 2 if (n // ring) % 2 == 0 and size % 256 == 0 else 1
    chunks = 2 * halves if size % (256 * halves) == 0 else halves
    return chunks, halves


def kernel(
    n, ring, c_ref, amp_ref, plan_ref, out_ref,
    cw, vw, vis, scaled, amps, amp_in, plan_in, own, sum_in, sum_out, s0, pieces, folded, wide,
    local_sem, cw_send, cw_recv, vw_send, vw_recv, sum_send, sum_recv, vis_send, vis_recv,
    piece_send, piece_recv, throw_send, serve_send, serve_recv, near_send, relay_send, pair_send, folded_recv,
):
    det = lax.axis_index("det")
    row = lax.axis_index("row")
    rows, size = out_ref.shape
    width = pieces.shape[2]
    per_block = n // ring
    chips = n // 2
    chip, core = det // 2, lax.rem(det, 2)
    partner = chip * 2 + (1 - core)
    even = core == 0
    quad = chips == 4 and per_block == 2
    home, corner = det // per_block, chips - 1 - chip
    served = ring >= 4
    reach = ring - 2 if served else ring - 1
    at_end = (row == 0) | (row == ring - 1)
    serves = even & ((row == 1) | (row == ring - 2))
    throws = (row == home) & ((row == 0) | (row == ring - 1))
    toward = (row < ring - 1, row > 0)
    sum_parts = parts_of(own.shape[0], 4)
    n_chunks, n_halves = splits(n, ring, size)
    chunk, half_size = size // n_chunks, size // n_halves

    def remote(src, dst, send, recv, **where):
        return pltpu.make_async_remote_copy(
            src_ref=src, dst_ref=dst, send_sem=send, recv_sem=recv,
            device_id=where, device_id_type=pl.DeviceIdType.MESH,
        )

    stage = [
        pltpu.make_async_copy(c_ref, cw.at[row], local_sem.at[0]),
        pltpu.make_async_copy(amp_ref, amp_in, local_sem.at[1]),
        pltpu.make_async_copy(plan_ref, plan_in, local_sem.at[2]),
    ]
    for copy in stage:
        copy.start()

    barrier = pltpu.get_barrier_semaphore()

    def greet(i):
        peer = lax.rem(det + 1 + i, n)
        pl.semaphore_signal(barrier, inc=1, device_id={"det": peer}, device_id_type=pl.DeviceIdType.MESH)

    each(n - 1, greet)

    for side in (0, 1):

        @pl.when(toward[side])
        def _():
            peer = row + 1 - 2 * side
            pl.semaphore_signal(barrier, inc=1, device_id={"row": peer}, device_id_type=pl.DeviceIdType.MESH)

    for copy in stage:
        copy.wait()
    amps[0] = jnp.broadcast_to(amp_in[...].astype(F32), amps.shape[1:])
    s0[...] = against(cw[row], cw[row])
    pl.semaphore_wait(barrier, n - 1 + toward[0].astype(jnp.int32) + toward[1].astype(jnp.int32))

    def along(block, side, q):
        span = cw.at[block, :, pl.ds(q * chunk, chunk)]
        return remote(
            span, span, cw_send.at[block, side, q], cw_recv.at[block, q], row=row + 1 - 2 * side
        )

    def pass_on(block, side, q, wait=False):
        @pl.when(toward[side])
        def _():
            copy = along(block, side, q)
            if wait:
                copy.wait_send()
            else:
                copy.start()

    def sum_copy(k, side):
        span = pl.ds(*sum_parts[k])
        return remote(
            sum_out.at[side, span], sum_in.at[side, span], sum_send.at[side, k], sum_recv.at[side, k],
            row=row + 1 - 2 * side,
        )

    def sums(side, distance):
        for k, (start, length) in enumerate(sum_parts):
            span = pl.ds(start, length)
            if distance:
                sum_copy(k, side).wait_recv()
            if distance < reach:
                sum_out[side, span] = own[span] + sum_in[side, span] if distance else own[span]
                sum_copy(k, side).start()

    def gather_sums(distance):
        if distance > reach:
            return

        @pl.when(even & (row == distance))
        def _():
            sums(0, distance)

        @pl.when(even & (row == ring - 1 - distance))
        def _():
            sums(1, distance)

    def piece(block, k):
        target = block * per_block + k
        start = pl.multiple_of(k * rows // width * width, width)
        return target, remote(
            cw.at[block, :, pl.ds(start, width)], pieces.at[det],
            piece_send.at[block, k], piece_recv.at[det], det=target,
        )

    def hand_out(block, half, wait=False):
        share = per_block // n_halves

        def one(i):
            target, copy = piece(block, half * share + i)

            direct = target != det
            if quad:
                direct &= (jnp.abs(block - row) < ring - 1) | (corner != block)

            @pl.when(direct)
            def _():
                if wait:
                    copy.wait_send()
                else:
                    copy.start()

        each(share, one)

    def thrown(i, wait=False):
        source = corner * 2 + i
        copy = remote(
            pieces.at[source], pieces.at[source], throw_send.at[i], piece_recv.at[source],
            row=ring - 1 - row,
        )

        @pl.when(throws)
        def _():
            if wait:
                copy.wait_send()
            else:
                copy.wait_recv()
                copy.start()

    def columns(ref, block, half):
        return ref[block, :, pl.ds(half * half_size, half_size)]

    def to_partner(block, half):
        span = pl.ds(half * half_size, half_size)
        return remote(
            cw.at[block, :, span], vw.at[block, :, span], vw_send.at[block, half], vw_recv.at[block, half],
            det=partner,
        )

    following = lax.rem(det + 1, n)
    visit = remote(cw.at[row], vis, vis_send.at[0], vis_recv.at[0], det=following)
    visit_amp = remote(amps.at[0], amps.at[1], vis_send.at[1], vis_recv.at[1], det=following)
    visit.start()
    visit_amp.start()
    for q in range(n_chunks):
        for side in (0, 1):
            pass_on(row, side, q)
    visit.wait_recv()
    own[...] = against(vis[...], cw[row])
    gather_sums(0)
    for half in range(n_halves):
        hand_out(row, half)

    def blocks_at(distance):
        for side in (0, 1):
            block = row - distance if side == 0 else row + distance
            yield side, block, (block >= 0) & (block < ring)

    def arrive(distance):
        for q in range(n_chunks):
            for side, block, there in blocks_at(distance):

                @pl.when(there)
                def _():
                    along(block, side, q).wait_recv()
                    pass_on(block, side, q)
                    if (q + 1) % (n_chunks // n_halves) == 0:
                        half = q // (n_chunks // n_halves)

                        @pl.when(even)
                        def _():
                            to_partner(block, half).start()

                        hand_out(block, half)
                        part = columns(cw, block, half)
                        s0[...] += against(part, part)

    def visited(distance):
        for half in range(n_halves):
            for side, block, there in blocks_at(distance):

                @pl.when(there & jnp.logical_not(even))
                def _():
                    to_partner(block, half).wait_recv()
                    own[...] += against(columns(vw, block, half), columns(cw, block, half))

    for distance in range(1, ring):
        arrive(distance)
        if distance < ring - 1:
            visited(distance)
            gather_sums(distance)
    visit_amp.wait_recv()
    amp = amps[0, 0:1, 0:1]
    masks = plan_in[...].astype(F32)
    is_served = even & at_end if served else jnp.bool_(False)
    serve = remote(scaled.at[1], scaled.at[1], serve_send, serve_recv, row=jnp.where(row == 1, 0, ring - 1))

    def scale_visitor():
        for side in (0, 1):

            @pl.when(even & toward[1 - side])
            def _():
                own[...] += sum_in[side]

        weight = amps[1, 0:1, 0:1] * amp * masks[0:1, 1:2]
        scaled[1] = (weight * inverse_of(own[...])).astype(BF16)

    if served:

        @pl.when(serves)
        def _():
            scale_visitor()
            serve.start()

    weight = amp * amp * masks[0:1, 0:1]
    scaled[0] = (weight * inverse_of(s0[...])).astype(BF16)
    total = jnp.dot(scaled[0], cw[row], preferred_element_type=F32)
    visited(ring - 1)
    gather_sums(ring - 1)
    pl.when(jnp.logical_not(is_served | serves) if served else jnp.bool_(True))(scale_visitor)
    if served:
        pl.when(is_served)(serve.wait_recv)

    def fold(half):
        start = half * half_size
        part = jnp.dot(scaled[1], vis[:, start : start + half_size], preferred_element_type=F32)
        folded[det, :, span_of(half)] = (total[:, start : start + half_size] + part).astype(BF16)

    def span_of(half):
        return pl.ds(half * half_size, half_size)

    def send_folded(source, half, target, send):
        span = folded.at[source, :, span_of(half)]
        return remote(span, span, send, folded_recv.at[source, half], det=target)

    def to_pair(source, half):
        return send_folded(source, half, partner, pair_send.at[source, half])

    def landed(source, half):
        to_pair(source, half).wait_recv()

    sink = out_ref if width == rows else wide

    def piece_here(source):
        remote(
            cw.at[0, :, pl.ds(0, width)], pieces.at[source], piece_send.at[0, 0], piece_recv.at[source],
            det=partner,
        ).wait_recv()

    def add(source, half):
        sink[:, span_of(half)] += gram(pieces[source], folded[source, :, span_of(half)])

    def add_own():
        own_start = lax.rem(det, per_block) * rows // width * width
        mine = cw[det // per_block, :, pl.ds(pl.multiple_of(own_start, width), width)]
        sink[...] = gram(mine, folded[det])
        piece_here(partner)
        for half in range(n_halves):
            landed(partner, half)
            add(partner, half)

    def arrived(source, half, then=None):
        landed(source, half)
        if then is not None:
            then()
        to_pair(source, half).start()

    def foreign(source, half, detoured=False):
        if half == 0:

            @pl.when(jnp.logical_not(detoured & throws))
            def _():
                piece_here(source)

        add(source, half)

    halves = range(n_halves)
    if quad:
        across_x = chip + 1 - 2 * lax.rem(chip, 2)
        across_y = lax.rem(chip + 2, 4)
        far = corner * 2
        first = jnp.where(even, across_x, across_y) * 2
        second = jnp.where(even, across_y, across_x) * 2

        def near(which, half):
            target = (first if which == 0 else second) + core
            return send_folded(det, half, target, near_send.at[which, half])

        def relay(half):
            return send_folded(first + core, half, second + core, relay_send.at[half])

        def across(half):
            return send_folded(det, half, far + core, relay_send.at[half])

        for half in halves:
            fold(half)
            near(0, half).start()
        for half in halves:
            to_pair(det, half).start()
        add_own()
        for half in halves:
            near(1, half).start()
        thrown(0)
        thrown(1)
        for half in halves:
            arrived(first + core, half, relay(half).start)
        for half in halves:
            foreign(first + core, half)
        for half in halves:
            arrived(second + core, half)
        for half in halves:
            foreign(second + core, half)
        for other in (second, first):
            for half in halves:
                landed(other + 1 - core, half)
                foreign(other + 1 - core, half)
        for half in halves:
            arrived(far + core, half)
            foreign(far + core, half, True)
        for half in halves:
            landed(far + 1 - core, half)
            foreign(far + 1 - core, half, True)
        for half in halves:
            near(0, half).wait_send()
            near(1, half).wait_send()
            relay(half).wait_send()
            for source in (det, first + core, second + core, far + core):
                to_pair(source, half).wait_send()
        thrown(0, wait=True)
        thrown(1, wait=True)
    else:

        def to_chip(i, half):
            target = lax.rem(chip + 1 + i, chips) * 2 + core
            return send_folded(det, half, target, near_send.at[i, half])

        def other(i):
            return lax.rem(chip + chips - 1 - i, chips) * 2

        def relay_all(i):
            for half in halves:
                arrived(other(i) + core, half)
                foreign(other(i) + core, half)

        def relayed(i):
            for half in halves:
                landed(other(i) + 1 - core, half)
                foreign(other(i) + 1 - core, half)

        for half in halves:
            fold(half)
            each(chips - 1, lambda i: to_chip(i, half).start())
            to_pair(det, half).start()
        add_own()
        each(chips - 1, relay_all)
        each(chips - 1, relayed)
        for half in halves:
            each(chips - 1, lambda i: to_chip(i, half).wait_send())
            to_pair(det, half).wait_send()
            each(chips - 1, lambda i: to_pair(other(i) + core, half).wait_send())
    if width != rows:
        out_ref[...] = wide[pl.ds(pl.multiple_of(lax.rem(det * rows, width), rows), rows)]

    if served:
        pl.when(serves)(serve.wait_send)
    visit.wait_send()
    visit_amp.wait_send()
    for side in (0, 1):
        for q in range(n_chunks):
            pass_on(row, side, q, wait=True)

        passed = row < reach if side == 0 else row > ring - 1 - reach

        @pl.when(even & passed)
        def _():
            for k in range(len(sum_parts)):
                sum_copy(k, side).wait_send()

    for half in halves:
        hand_out(row, half, wait=True)
    for distance in range(1, ring):
        for side, block, there in blocks_at(distance):

            @pl.when(there)
            def _():
                for q in range(n_chunks):
                    pass_on(block, side, q, wait=True)
                for half in halves:
                    hand_out(block, half, wait=True)

            @pl.when(there & even)
            def _():
                for half in halves:
                    to_partner(block, half).wait_send()


def on_device(coefficients, amplitudes, plan):
    n, ring = lax.axis_size("det"), lax.axis_size("row")
    if coefficients.shape[0] != 1 or plan.shape[1] != 2:
        raise ValueError("unsupported sizes")
    block = jnp.swapaxes(coefficients, 1, 2)[0]
    orbitals, size = block.shape
    rows = size * ring // n
    width = max(rows, 128)
    chunks, halves = splits(n, ring, size)
    dma = pltpu.SemaphoreType.DMA
    lanes = -(-orbitals // 128) * 128
    used = 2 * orbitals * (size * (2 * ring + 1 + n) + width * n) + 28 * orbitals * lanes + 4 * size * (rows + width)
    return pl.pallas_call(
        functools.partial(kernel, n, ring),
        out_shape=jax.ShapeDtypeStruct((rows, size), F32),
        in_specs=[pl.BlockSpec(memory_space=pltpu.HBM)] * 3,
        out_specs=pl.BlockSpec(memory_space=pltpu.VMEM),
        scratch_shapes=[
            pltpu.VMEM((ring, orbitals, size), BF16),
            pltpu.VMEM((ring, orbitals, size), BF16),
            pltpu.VMEM((orbitals, size), BF16),
            pltpu.VMEM((2, orbitals, orbitals), BF16),
            pltpu.VMEM((2, 8, 128), F32),
            pltpu.VMEM((1, 1), amplitudes.dtype),
            pltpu.VMEM((1, 2), plan.dtype),
            pltpu.VMEM((orbitals, orbitals), F32),
            pltpu.VMEM((2, orbitals, orbitals), F32),
            pltpu.VMEM((2, orbitals, orbitals), F32),
            pltpu.VMEM((orbitals, orbitals), F32),
            pltpu.VMEM((n, orbitals, width), BF16),
            pltpu.VMEM((n, orbitals, size), BF16),
            pltpu.VMEM((width, size) if width != rows else (8, 128), F32),
            dma((3,)), dma((ring, 2, chunks)), dma((ring, chunks)), dma((ring, halves)), dma((ring, halves)),
            dma((2, 4)), dma((2, 4)), dma((2,)), dma((2,)), dma((ring, n // ring)), dma((n,)), dma((2,)), dma, dma,
            dma((n // 2, halves)), dma((halves,)), dma((n, halves)), dma((n, halves)),
        ],
        compiler_params=pltpu.CompilerParams(
            collective_id=0, has_side_effects=True, vmem_limit_bytes=used + 4 * 1024 * 1024
        ),
    )(
        pltpu.with_memory_space_constraint(block, pltpu.HBM),
        amplitudes.reshape(1, 1),
        pltpu.with_memory_space_constraint(jnp.swapaxes(plan, 1, 2).reshape(1, 2), pltpu.HBM),
    )


def solution(mesh):
    placed = (P("det", "row", None), P("det"), P("det", None, None))
    return jax.shard_map(
        on_device, mesh=mesh, in_specs=placed, out_specs=P("det", "row"), check_vma=False
    )
```

```python
import functools

import jax
import jax.numpy as jnp
from jax import lax
from jax.experimental import pallas as pl
from jax.experimental.pallas import tpu as pltpu
from jax.sharding import PartitionSpec as P

ORDER = 2
F32 = jnp.float32
BF16 = jnp.bfloat16


def each(count, body):
    if count <= 8:
        for i in range(count):
            body(i)
    else:
        lax.fori_loop(0, count, lambda i, c: (body(i), c)[1], 0)


def inverse_of(correlation):
    size = correlation.shape[0]
    row = lax.broadcasted_iota(jnp.int32, (size, size), 0)
    col = lax.broadcasted_iota(jnp.int32, (size, size), 1)
    identity = jnp.where(row == col, 1.0, 0.0).astype(F32)
    remainder = identity - correlation
    inverse = identity + remainder
    for level in range(ORDER - 1):
        inverse = identity + jnp.dot(
            remainder, inverse, precision=lax.Precision.HIGHEST, preferred_element_type=F32
        )
    return inverse


def gram(a, b):
    return lax.dot_general(a, b, (((0,), (0,)), ((), ())), preferred_element_type=F32)


def against(a, b):
    return lax.dot_general(a, b, (((1,), (1,)), ((), ())), preferred_element_type=F32)


def parts_of(size, count):
    step = -(-size // (8 * count)) * 8
    return [(start, min(step, size - start)) for start in range(0, size, step)]


def splits(n, ring, size):
    halves = 2 if (n // ring) % 2 == 0 and size % 256 == 0 else 1
    chunks = 2 * halves if size % (256 * halves) == 0 else halves
    return chunks, halves


def kernel(
    n, ring, c_ref, amp_ref, plan_ref, out_ref,
    cw, vw, vis, scaled, amps, amp_in, plan_in, own, sum_in, sum_out, s0, pieces, folded, wide,
    local_sem, cw_send, cw_recv, vw_send, vw_recv, sum_send, sum_recv, vis_send, vis_recv,
    piece_send, piece_recv, throw_send, serve_send, serve_recv, near_send, relay_send, pair_send, folded_recv,
):
    det = lax.axis_index("det")
    row = lax.axis_index("row")
    rows, size = out_ref.shape
    width = pieces.shape[2]
    per_block = n // ring
    chips = n // 2
    chip, core = det // 2, lax.rem(det, 2)
    partner = chip * 2 + (1 - core)
    even = core == 0
    quad = chips == 4 and per_block == 2
    home, corner = det // per_block, chips - 1 - chip
    served = ring >= 4
    reach = ring - 2 if served else ring - 1
    at_end = (row == 0) | (row == ring - 1)
    serves = even & ((row == 1) | (row == ring - 2))
    throws = (row == home) & ((row == 0) | (row == ring - 1))
    toward = (row < ring - 1, row > 0)
    sum_parts = parts_of(own.shape[0], 4)
    n_chunks, n_halves = splits(n, ring, size)
    chunk, half_size = size // n_chunks, size // n_halves

    def remote(src, dst, send, recv, **where):
        return pltpu.make_async_remote_copy(
            src_ref=src, dst_ref=dst, send_sem=send, recv_sem=recv,
            device_id=where, device_id_type=pl.DeviceIdType.MESH,
        )

    barrier = pltpu.get_barrier_semaphore()

    def greet(i):
        peer = lax.rem(det + 1 + i, n)
        pl.semaphore_signal(barrier, inc=1, device_id={"det": peer}, device_id_type=pl.DeviceIdType.MESH)

    each(n - 1, greet)

    for side in (0, 1):

        @pl.when(toward[side])
        def _():
            peer = row + 1 - 2 * side
            pl.semaphore_signal(barrier, inc=1, device_id={"row": peer}, device_id_type=pl.DeviceIdType.MESH)

    stage = [
        pltpu.make_async_copy(c_ref, cw.at[row], local_sem.at[0]),
        pltpu.make_async_copy(amp_ref, amp_in, local_sem.at[1]),
        pltpu.make_async_copy(plan_ref, plan_in, local_sem.at[2]),
    ]
    for copy in stage:
        copy.start()

    for copy in stage:
        copy.wait()
    amps[0] = jnp.broadcast_to(amp_in[...].astype(F32), amps.shape[1:])
    s0[...] = against(cw[row], cw[row])
    pl.semaphore_wait(barrier, n - 1 + toward[0].astype(jnp.int32) + toward[1].astype(jnp.int32))

    def along(block, side, q):
        span = cw.at[block, :, pl.ds(q * chunk, chunk)]
        return remote(
            span, span, cw_send.at[block, side, q], cw_recv.at[block, q], row=row + 1 - 2 * side
        )

    def pass_on(block, side, q, wait=False):
        @pl.when(toward[side])
        def _():
            copy = along(block, side, q)
            if wait:
                copy.wait_send()
            else:
                copy.start()

    def sum_copy(k, side):
        span = pl.ds(*sum_parts[k])
        return remote(
            sum_out.at[side, span], sum_in.at[side, span], sum_send.at[side, k], sum_recv.at[side, k],
            row=row + 1 - 2 * side,
        )

    def sums(side, distance):
        for k, (start, length) in enumerate(sum_parts):
            span = pl.ds(start, length)
            if distance:
                sum_copy(k, side).wait_recv()
            if distance < reach:
                sum_out[side, span] = own[span] + sum_in[side, span] if distance else own[span]
                sum_copy(k, side).start()

    def gather_sums(distance):
        if distance > reach:
            return

        @pl.when(even & (row == distance))
        def _():
            sums(0, distance)

        @pl.when(even & (row == ring - 1 - distance))
        def _():
            sums(1, distance)

    def piece(block, k):
        target = block * per_block + k
        start = pl.multiple_of(k * rows // width * width, width)
        return target, remote(
            cw.at[block, :, pl.ds(start, width)], pieces.at[det],
            piece_send.at[block, k], piece_recv.at[det], det=target,
        )

    def hand_out(block, half, wait=False):
        share = per_block // n_halves

        def one(i):
            target, copy = piece(block, half * share + i)

            direct = target != det
            if quad:
                direct &= (jnp.abs(block - row) < ring - 1) | (corner != block)

            @pl.when(direct)
            def _():
                if wait:
                    copy.wait_send()
                else:
                    copy.start()

        each(share, one)

    def thrown(i, wait=False):
        source = corner * 2 + i
        copy = remote(
            pieces.at[source], pieces.at[source], throw_send.at[i], piece_recv.at[source],
            row=ring - 1 - row,
        )

        @pl.when(throws)
        def _():
            if wait:
                copy.wait_send()
            else:
                copy.wait_recv()
                copy.start()

    def columns(ref, block, half):
        return ref[block, :, pl.ds(half * half_size, half_size)]

    def to_partner(block, half):
        span = pl.ds(half * half_size, half_size)
        return remote(
            cw.at[block, :, span], vw.at[block, :, span], vw_send.at[block, half], vw_recv.at[block, half],
            det=partner,
        )

    following = lax.rem(det + 1, n)
    visit = remote(cw.at[row], vis, vis_send.at[0], vis_recv.at[0], det=following)
    visit_amp = remote(amps.at[0], amps.at[1], vis_send.at[1], vis_recv.at[1], det=following)
    visit.start()
    visit_amp.start()
    for q in range(n_chunks):
        for side in (0, 1):
            pass_on(row, side, q)
    visit.wait_recv()
    own[...] = against(vis[...], cw[row])
    gather_sums(0)
    for half in range(n_halves):
        hand_out(row, half)

    def blocks_at(distance):
        for side in (0, 1):
            block = row - distance if side == 0 else row + distance
            yield side, block, (block >= 0) & (block < ring)

    def arrive(distance):
        for q in range(n_chunks):
            for side, block, there in blocks_at(distance):

                @pl.when(there)
                def _():
                    along(block, side, q).wait_recv()
                    pass_on(block, side, q)
                    if (q + 1) % (n_chunks // n_halves) == 0:
                        half = q // (n_chunks // n_halves)

                        @pl.when(even)
                        def _():
                            to_partner(block, half).start()

                        hand_out(block, half)
                        part = columns(cw, block, half)
                        s0[...] += against(part, part)

    def visited(distance):
        for half in range(n_halves):
            for side, block, there in blocks_at(distance):

                @pl.when(there & jnp.logical_not(even))
                def _():
                    to_partner(block, half).wait_recv()
                    own[...] += against(columns(vw, block, half), columns(cw, block, half))

    for distance in range(1, ring):
        arrive(distance)
        if distance < ring - 1:
            visited(distance)
            gather_sums(distance)
    visit_amp.wait_recv()
    amp = amps[0, 0:1, 0:1]
    masks = plan_in[...].astype(F32)
    is_served = even & at_end if served else jnp.bool_(False)
    serve = remote(scaled.at[1], scaled.at[1], serve_send, serve_recv, row=jnp.where(row == 1, 0, ring - 1))

    def scale_visitor():
        for side in (0, 1):

            @pl.when(even & toward[1 - side])
            def _():
                own[...] += sum_in[side]

        weight = amps[1, 0:1, 0:1] * amp * masks[0:1, 1:2]
        scaled[1] = (weight * inverse_of(own[...])).astype(BF16)

    if served:

        @pl.when(serves)
        def _():
            scale_visitor()
            serve.start()

    weight = amp * amp * masks[0:1, 0:1]
    scaled[0] = (weight * inverse_of(s0[...])).astype(BF16)
    total = jnp.dot(scaled[0], cw[row], preferred_element_type=F32)
    visited(ring - 1)
    gather_sums(ring - 1)
    pl.when(jnp.logical_not(is_served | serves) if served else jnp.bool_(True))(scale_visitor)
    if served:
        pl.when(is_served)(serve.wait_recv)
    total = total + jnp.dot(scaled[1], vis[...], preferred_element_type=F32)
    folded[det] = total.astype(BF16)

    def span_of(half):
        return pl.ds(half * half_size, half_size)

    def send_folded(source, half, target, send):
        span = folded.at[source, :, span_of(half)]
        return remote(span, span, send, folded_recv.at[source, half], det=target)

    def to_pair(source, half):
        return send_folded(source, half, partner, pair_send.at[source, half])

    def landed(source, half):
        to_pair(source, half).wait_recv()

    sink = out_ref if width == rows else wide

    def piece_here(source):
        remote(
            cw.at[0, :, pl.ds(0, width)], pieces.at[source], piece_send.at[0, 0], piece_recv.at[source],
            det=partner,
        ).wait_recv()

    def add(source, half):
        sink[:, span_of(half)] += gram(pieces[source], folded[source, :, span_of(half)])

    def add_own():
        own_start = lax.rem(det, per_block) * rows // width * width
        mine = cw[det // per_block, :, pl.ds(pl.multiple_of(own_start, width), width)]
        sink[...] = gram(mine, folded[det])
        piece_here(partner)
        for half in range(n_halves):
            landed(partner, half)
            add(partner, half)

    def arrived(source, half, then=None):
        landed(source, half)
        if then is not None:
            then()
        to_pair(source, half).start()

    def foreign(source, half, detoured=False):
        if half == 0:

            @pl.when(jnp.logical_not(detoured & throws))
            def _():
                piece_here(source)

        add(source, half)

    halves = range(n_halves)
    if quad:
        across_x = chip + 1 - 2 * lax.rem(chip, 2)
        across_y = lax.rem(chip + 2, 4)
        far = corner * 2
        first = jnp.where(even, across_x, across_y) * 2
        second = jnp.where(even, across_y, across_x) * 2

        def near(which, half):
            target = (first if which == 0 else second) + core
            return send_folded(det, half, target, near_send.at[which, half])

        def relay(half):
            return send_folded(first + core, half, second + core, relay_send.at[half])

        def across(half):
            return send_folded(det, half, far + core, relay_send.at[half])

        for half in halves:
            near(0, half).start()
        for half in halves:
            to_pair(det, half).start()
        add_own()
        for half in halves:
            near(1, half).start()
        thrown(0)
        thrown(1)
        for half in halves:
            arrived(first + core, half, relay(half).start)
        for half in halves:
            foreign(first + core, half)
        for half in halves:
            arrived(second + core, half)
        for half in halves:
            foreign(second + core, half)
        for other in (second, first):
            for half in halves:
                landed(other + 1 - core, half)
                foreign(other + 1 - core, half)
        for half in halves:
            arrived(far + core, half)
            foreign(far + core, half, True)
        for half in halves:
            landed(far + 1 - core, half)
            foreign(far + 1 - core, half, True)
        for half in halves:
            near(0, half).wait_send()
            near(1, half).wait_send()
            relay(half).wait_send()
            for source in (det, first + core, second + core, far + core):
                to_pair(source, half).wait_send()
        thrown(0, wait=True)
        thrown(1, wait=True)
    else:

        def to_chip(i, half):
            target = lax.rem(chip + 1 + i, chips) * 2 + core
            return send_folded(det, half, target, near_send.at[i, half])

        def other(i):
            return lax.rem(chip + chips - 1 - i, chips) * 2

        def relay_all(i):
            for half in halves:
                arrived(other(i) + core, half)
                foreign(other(i) + core, half)

        def relayed(i):
            for half in halves:
                landed(other(i) + 1 - core, half)
                foreign(other(i) + 1 - core, half)

        for half in halves:
            each(chips - 1, lambda i: to_chip(i, half).start())
            to_pair(det, half).start()
        add_own()
        each(chips - 1, relay_all)
        each(chips - 1, relayed)
        for half in halves:
            each(chips - 1, lambda i: to_chip(i, half).wait_send())
            to_pair(det, half).wait_send()
            each(chips - 1, lambda i: to_pair(other(i) + core, half).wait_send())
    if width != rows:
        out_ref[...] = wide[pl.ds(pl.multiple_of(lax.rem(det * rows, width), rows), rows)]

    if served:
        pl.when(serves)(serve.wait_send)
    visit.wait_send()
    visit_amp.wait_send()
    for side in (0, 1):
        for q in range(n_chunks):
            pass_on(row, side, q, wait=True)

        passed = row < reach if side == 0 else row > ring - 1 - reach

        @pl.when(even & passed)
        def _():
            for k in range(len(sum_parts)):
                sum_copy(k, side).wait_send()

    for half in halves:
        hand_out(row, half, wait=True)
    for distance in range(1, ring):
        for side, block, there in blocks_at(distance):

            @pl.when(there)
            def _():
                for q in range(n_chunks):
                    pass_on(block, side, q, wait=True)
                for half in halves:
                    hand_out(block, half, wait=True)

            @pl.when(there & even)
            def _():
                for half in halves:
                    to_partner(block, half).wait_send()


def on_device(coefficients, amplitudes, plan):
    n, ring = lax.axis_size("det"), lax.axis_size("row")
    if coefficients.shape[0] != 1 or plan.shape[1] != 2:
        raise ValueError("unsupported sizes")
    block = jnp.swapaxes(coefficients, 1, 2)[0]
    orbitals, size = block.shape
    rows = size * ring // n
    width = max(rows, 128)
    chunks, halves = splits(n, ring, size)
    dma = pltpu.SemaphoreType.DMA
    lanes = -(-orbitals // 128) * 128
    used = 2 * orbitals * (size * (2 * ring + 1 + n) + width * n) + 28 * orbitals * lanes + 4 * size * (rows + width)
    return pl.pallas_call(
        functools.partial(kernel, n, ring),
        out_shape=jax.ShapeDtypeStruct((rows, size), F32),
        in_specs=[pl.BlockSpec(memory_space=pltpu.HBM)] * 3,
        out_specs=pl.BlockSpec(memory_space=pltpu.VMEM),
        scratch_shapes=[
            pltpu.VMEM((ring, orbitals, size), BF16),
            pltpu.VMEM((ring, orbitals, size), BF16),
            pltpu.VMEM((orbitals, size), BF16),
            pltpu.VMEM((2, orbitals, orbitals), BF16),
            pltpu.VMEM((2, 8, 128), F32),
            pltpu.VMEM((1, 1), amplitudes.dtype),
            pltpu.VMEM((1, 2), plan.dtype),
            pltpu.VMEM((orbitals, orbitals), F32),
            pltpu.VMEM((2, orbitals, orbitals), F32),
            pltpu.VMEM((2, orbitals, orbitals), F32),
            pltpu.VMEM((orbitals, orbitals), F32),
            pltpu.VMEM((n, orbitals, width), BF16),
            pltpu.VMEM((n, orbitals, size), BF16),
            pltpu.VMEM((width, size) if width != rows else (8, 128), F32),
            dma((3,)), dma((ring, 2, chunks)), dma((ring, chunks)), dma((ring, halves)), dma((ring, halves)),
            dma((2, 4)), dma((2, 4)), dma((2,)), dma((2,)), dma((ring, n // ring)), dma((n,)), dma((2,)), dma, dma,
            dma((n // 2, halves)), dma((halves,)), dma((n, halves)), dma((n, halves)),
        ],
        compiler_params=pltpu.CompilerParams(
            collective_id=0, has_side_effects=True, vmem_limit_bytes=used + 4 * 1024 * 1024
        ),
    )(
        pltpu.with_memory_space_constraint(block, pltpu.HBM),
        amplitudes.reshape(1, 1),
        pltpu.with_memory_space_constraint(jnp.swapaxes(plan, 1, 2).reshape(1, 2), pltpu.HBM),
    )


def solution(mesh):
    placed = (P("det", "row", None), P("det"), P("det", None, None))
    return jax.shard_map(
        on_device, mesh=mesh, in_specs=placed, out_specs=P("det", "row"), check_vma=False
    )
```
